32 devices in a mesh: seq: 8 (over z, y), tp: 4 (over x, core).
Axes of the slice: x: 2, y: 2, z: 4, core: 2. Of those that a mesh axis runs over, the one named last changes fastest.
Arguments:
- tokens: bfloat16 [16384, 1024], P(('seq', 'tp')), may hold values from -6 to 6
- query_weight: bfloat16 [1024, 1024], replicated, may hold values from -0.1875 to 0.1875
- key_weight: bfloat16 [1024, 1024], replicated, may hold values from -0.1875 to 0.1875
- value_weight: bfloat16 [1024, 1024], replicated, may hold values from -0.1875 to 0.1875
- modulate_weight: bfloat16 [1024, 1024], replicated, may hold values from -0.1875 to 0.1875
- output_weight: bfloat16 [1024, 1024], replicated, may hold values from -0.1875 to 0.1875
- gate_weight: bfloat16 [1024, 2816], P(None, 'tp'), may hold values from -0.1875 to 0.1875
- linear_weight: bfloat16 [1024, 2816], P(None, 'tp'), may hold values from -0.1875 to 0.1875
- down_weight: bfloat16 [2816, 1024], P('tp'), may hold values from -0.109375 to 0.109375
- cotangent: bfloat16 [16384, 1024], P(('seq', 'tp')), may hold values from -6 to 6
- decay_exponent: int32 [8], replicated, may hold values from 5 to 17
Outputs:
- mixed: bfloat16 [16384, 1024], P(('seq', 'tp'))
- tokens_grad: float32 [16384, 1024], P(('seq', 'tp'))
- query_grad: float32 [1024, 1024], replicated
- key_grad: float32 [1024, 1024], replicated
- value_grad: float32 [1024, 1024], replicated
- modulate_grad: float32 [1024, 1024], replicated
- output_grad: float32 [1024, 1024], replicated
- gate_grad: float32 [1024, 2816], P('seq', 'tp')
- linear_grad: float32 [1024, 2816], P('seq', 'tp')
- down_grad: float32 [2816, 1024], P('tp', 'seq')
The draws below stay inside these ranges and needn't reach their ends.
Inputs may be any that keep to these rules, and one draw needn't show every extreme that they name: `decay_exponent`: head h decays by a factor 2 ** (-2 ** (-decay_exponent_h)) a token.
All inputs are finite; a program needn't handle non-finite values.
Results may differ from the reference program's by a relative error of at most 0.015.
Values may be sent and summed in bfloat16 or wider, within the bound.
No kernel may reach another device: no remote copies, remote signals or barrier semaphores. Data moves between devices by JAX's collectives and lax.ppermute only.
A program may use at most 320 MiB of HBM per device.

```python
import math
import jax
import jax.numpy as jnp
from jax import lax

WIDTH = 1024
HEADS = 8
HEAD_DIM = 128
INNER = 2816
BLOCK = 256
TOKENS = 16384
LENGTH = 16384


def set_ends(entries, key, low, top_value):
    spot = [jax.random.randint(jax.random.fold_in(key, axis), (), 0, length) for axis, length in enumerate(entries.shape)]
    longest = entries.shape.index(max(entries.shape))
    neighbour = spot[:longest] + [(spot[longest] + 1) % entries.shape[longest]] + spot[longest + 1:]
    return entries.at[tuple(spot)].set(low).at[tuple(neighbour)].set(top_value)


def steps_of(key, extent, shards, low, high):
    level, own = 1.0, jax.random.fold_in(key, 6)
    for dim, blocks in shards:
        heights = jnp.exp(jax.random.uniform(jax.random.fold_in(own, dim), (blocks,), jnp.float32, low / len(shards), high / len(shards)))
        level = level * jnp.repeat(heights, extent[dim] // blocks).reshape([-1 if axis == dim else 1 for axis in range(len(extent))])
    return level


def scatter_about(rng, shape, spread, reach, split=(), held_as=jnp.bfloat16):
    level = steps_of(rng, shape, split, -0.22, 0.18) if split else 1.0
    values = jax.random.normal(rng, shape, jnp.float32) * spread * level
    return jnp.minimum(jnp.maximum(values, -reach), reach).astype(held_as)


def setup_inputs(seed: int = 0) -> dict:
    splits = jax.random.split(jax.random.key(seed), 12)
    tokens = scatter_about(splits[0], (TOKENS, WIDTH), 1.0, 6.0, ((0, 32),))
    query_weight = scatter_about(splits[1], (WIDTH, WIDTH), WIDTH ** -0.5, 0.1875)
    key_weight = scatter_about(splits[2], (WIDTH, WIDTH), WIDTH ** -0.5, 0.1875)
    value_weight = scatter_about(splits[3], (WIDTH, WIDTH), WIDTH ** -0.5, 0.1875)
    modulate_weight = scatter_about(splits[4], (WIDTH, WIDTH), WIDTH ** -0.5, 0.1875)
    output_weight = scatter_about(splits[5], (WIDTH, WIDTH), WIDTH ** -0.5, 0.1875)
    gate_weight = scatter_about(splits[6], (WIDTH, INNER), WIDTH ** -0.5, 0.1875, ((1, 4),))
    linear_weight = scatter_about(splits[7], (WIDTH, INNER), WIDTH ** -0.5, 0.1875, ((1, 4),))
    down_weight = scatter_about(splits[8], (INNER, WIDTH), INNER ** -0.5, 0.109375, ((0, 4),))
    cotangent = scatter_about(splits[9], (TOKENS, WIDTH), 1.0, 6.0, ((0, 32),))
    decay_exponent = set_ends(jax.random.randint(splits[10], (HEADS,), 5, 18), jax.random.fold_in(splits[10], 1), 5, 17).astype(jnp.int32)
    return dict(tokens=tokens, query_weight=query_weight, key_weight=key_weight, value_weight=value_weight, modulate_weight=modulate_weight, output_weight=output_weight, gate_weight=gate_weight, linear_weight=linear_weight, down_weight=down_weight, cotangent=cotangent, decay_exponent=decay_exponent)


EPS = 1e-06
HIGH = lax.Precision.HIGHEST

@jax.custom_vjp
def low(v):
    return lax.optimization_barrier(v.astype(jnp.bfloat16)).astype(jnp.float32)

@jax.custom_vjp
def low_back(v):
    return v

def low_keep(v):
    return (low(v), None)

def low_pass(kept, grad):
    return (grad,)

def back_keep(v):
    return (v, None)

def back_low(kept, grad):
    return (low(grad),)
low.defvjp(low_keep, low_pass)
low_back.defvjp(back_keep, back_low)

def srms(values):
    return values * lax.rsqrt(lax.optimization_barrier(jnp.mean(values * values, axis=-1, keepdims=True)) + EPS)

def swish(values):
    return values * jax.nn.sigmoid(values)

def dense(left, right):
    return jnp.dot(left, right, precision=HIGH)

def angles(position, halves):
    column = jnp.arange(halves, dtype=jnp.int32)
    factor = 1 + jnp.right_shift(jnp.full((halves,), 16384, jnp.int32), column // 4)
    phase = position[:, None] * factor[None, :] % 65536
    turned = phase.astype(jnp.float32) * (2.0 * math.pi / 65536.0)
    return (jnp.cos(turned)[:, None, :], jnp.sin(turned)[:, None, :])

def rotate(values, cosine, sine):
    halves = values.shape[-1] // 2
    first = values[..., :halves]
    second = values[..., halves:]
    return jnp.concatenate([first * cosine - second * sine, first * sine + second * cosine], axis=-1)

def layer(inputs, weights, decay_rate, cosine, sine):
    query_weight, key_weight, value_weight, modulate_weight, output_weight, gate_weight, linear_weight, down_weight = weights
    length = inputs.shape[0]
    normed = low(srms(inputs))
    pre_query = low_back(dense(normed, query_weight))
    pre_key = low_back(dense(normed, key_weight))
    query = low(rotate(swish(pre_query).reshape(length, HEADS, HEAD_DIM), cosine, sine))
    keys = low(rotate(swish(pre_key).reshape(length, HEADS, HEAD_DIM), cosine, sine))
    values = low(low_back(dense(normed, value_weight))).reshape(length, HEADS, HEAD_DIM)
    modulate = low_back(dense(normed, modulate_weight))
    offsets = jnp.arange(BLOCK, dtype=jnp.float32)
    distance = offsets[:, None] - offsets[None, :]
    decay_matrix = jnp.where(distance[None] >= 0.0, jnp.exp2(-jnp.maximum(distance, 0.0)[None] * decay_rate[:, None, None]), 0.0)
    query_decay = jnp.exp2(-(offsets + 1.0)[:, None] * decay_rate[None, :])[:, :, None]
    key_decay = jnp.exp2(-(BLOCK - 1.0 - offsets)[:, None] * decay_rate[None, :])[:, :, None]
    block_decay = jnp.exp2(-BLOCK * decay_rate)[:, None, None]

    def block_step(state, block):
        block_query, block_key, block_value = block
        scores = low_back(jnp.einsum('ihd,jhd->hij', block_query, block_key, precision=HIGH))
        probs = low(scores * decay_matrix)
        intra = jnp.einsum('hij,jhd->ihd', probs, block_value, precision=HIGH)
        decayed_query = low(block_query * query_decay)
        decayed_key = low(block_key * key_decay)
        inter = jnp.einsum('ihd,hde->ihe', decayed_query, low(state), precision=HIGH)
        contrib = jnp.einsum('jhd,jhe->hde', decayed_key, block_value, precision=HIGH)
        return (block_decay * state + contrib, intra + inter)
    blocks = length // BLOCK
    stacked = (query.reshape(blocks, BLOCK, HEADS, HEAD_DIM), keys.reshape(blocks, BLOCK, HEADS, HEAD_DIM), values.reshape(blocks, BLOCK, HEADS, HEAD_DIM))
    start_state = jnp.zeros((HEADS, HEAD_DIM, HEAD_DIM), jnp.float32)
    final_state, attended = lax.scan(jax.checkpoint(block_step), start_state, stacked)
    attended = low_back(attended.reshape(length, WIDTH))
    gated = low(srms(attended) * modulate)
    resid = inputs + low_back(dense(gated, output_weight))
    normed_two = low(srms(resid))
    gate_pre = low_back(dense(normed_two, gate_weight))
    linear_pre = low_back(dense(normed_two, linear_weight))
    hidden = low(gate_pre * linear_pre)
    return resid + dense(hidden, down_weight)

def reference(tokens, query_weight, key_weight, value_weight, modulate_weight, output_weight, gate_weight, linear_weight, down_weight, cotangent, decay_exponent):
    weights = (query_weight.astype(jnp.float32), key_weight.astype(jnp.float32), value_weight.astype(jnp.float32), modulate_weight.astype(jnp.float32), output_weight.astype(jnp.float32), gate_weight.astype(jnp.float32), linear_weight.astype(jnp.float32), down_weight.astype(jnp.float32))
    decay_rate = jnp.exp2(-decay_exponent.astype(jnp.float32))
    position = jnp.arange(LENGTH, dtype=jnp.int32)
    cosine, sine = angles(position, HEAD_DIM // 2)
    count = TOKENS // LENGTH
    seq_inputs = tokens.astype(jnp.float32).reshape(count, LENGTH, WIDTH)
    seq_cot = cotangent.astype(jnp.float32).reshape(count, LENGTH, WIDTH)

    def one_sequence(totals, paired):
        inputs, cot_rows = paired

        def forward(inputs, weights):
            return layer(inputs, weights, decay_rate, cosine, sine)
        mixed, pullback = jax.vjp(forward, inputs, weights)
        input_grad, weight_grads = pullback(cot_rows)
        totals = jax.tree.map(lambda first, second: first + second, totals, weight_grads)
        return (totals, (mixed, input_grad))
    zeros = jax.tree.map(jnp.zeros_like, weights)
    totals, outputs = lax.scan(one_sequence, zeros, (seq_inputs, seq_cot))
    mixed = outputs[0].reshape(TOKENS, WIDTH).astype(jnp.bfloat16)
    tokens_grad = outputs[1].reshape(TOKENS, WIDTH)
    return (mixed, tokens_grad, totals[0], totals[1], totals[2], totals[3], totals[4], totals[5], totals[6], totals[7])
```

```python
import math

import jax
import jax.numpy as jnp
from jax import lax
from jax.sharding import PartitionSpec as P

BLOCK = 256
SEQ_LEN = 16384


EPS = 1e-06
HIGH = lax.Precision.HIGHEST
FLOAT = jnp.float32
BHALF = jnp.bfloat16


def bits_of(count):
    return [1 << b for b in range(count.bit_length() - 1)]


def swap(value, mask, axes=("seq", "tp")):
    count = lax.axis_size(axes)
    return lax.ppermute(value, axes, [(s, s ^ mask) for s in range(count)])


def flat_place():
    return lax.axis_index("seq") * lax.axis_size("tp") + lax.axis_index("tp")


def bit_of(place, mask):
    return (place // mask) % 2


def halve(value, masks, place):
    for mask in masks:
        halves = value.reshape((2, value.shape[0] // 2) + value.shape[1:])
        bit = bit_of(place, mask)
        keep = lax.dynamic_index_in_dim(halves, bit, 0, False)
        send = lax.dynamic_index_in_dim(halves, 1 - bit, 0, False)
        value = (keep.astype(FLOAT) + swap(send.astype(BHALF), mask).astype(FLOAT)).astype(BHALF)
    return value


def double(value, masks, place):
    for mask in masks:
        other = swap(value, mask)
        bit = bit_of(place, mask)
        first = jnp.where(bit == 0, value, other)
        second = jnp.where(bit == 0, other, value)
        value = jnp.concatenate([first, second], axis=0)
    return value


def all_reduce(value, masks, place):
    part = halve(value, masks, place)
    return double(part, list(reversed(masks)), place).astype(FLOAT)


def decayed_scan(state, device_decay, span, place, reverse):
    heads = state.shape[0]
    half = heads // 2
    bit = bit_of(place, 1)
    halves = state.reshape((2, half) + state.shape[1:])
    mine = lax.dynamic_index_in_dim(halves, bit, 0, False)
    theirs = lax.dynamic_index_in_dim(halves, 1 - bit, 0, False)
    other = swap(theirs.astype(BHALF), 1).astype(FLOAT)
    decay = lax.dynamic_index_in_dim(device_decay.reshape(2, half), bit, 0, False)
    later = 1 - bit if reverse else bit

    def power(count):
        return (decay ** count)[:, None, None]

    core_later = jnp.where(later == 1, mine, other)
    core_first = jnp.where(later == 1, other, mine)
    total = power(1.0) * core_first + core_later
    prefix = jnp.zeros_like(total)
    for mask in bits_of(span)[1:]:
        bit = bit_of(place, mask)
        later = 1 - bit if reverse else bit
        got = swap(total.astype(BHALF), mask).astype(FLOAT)
        within = (place % mask) // 2
        if reverse:
            within = mask // 2 - 1 - within
        scale = power(2.0 * within.astype(FLOAT))
        prefix = prefix + jnp.where(later == 1, scale * got, 0.0)
        total = jnp.where(later == 1, power(float(mask)) * got + total, power(float(mask)) * total + got)
    first_pre = prefix
    second_pre = power(1.0) * prefix + core_first
    bit = bit_of(place, 1)
    later = 1 - bit if reverse else bit
    own = jnp.where(later == 1, second_pre, first_pre)
    away = jnp.where(later == 1, first_pre, second_pre)
    got = swap(away.astype(BHALF), 1).astype(FLOAT)
    low = jnp.where(bit == 0, own, got)
    high = jnp.where(bit == 0, got, own)
    return jnp.concatenate([low, high], axis=0)


def gather_group(value, masks):
    rows = {0: value}
    for mask in masks:
        for r in list(rows):
            rows[r | mask] = swap(rows[r], mask)
    return [rows[r] for r in range(len(rows))]


def scatter_group(parts, masks):
    parts = list(parts)
    rows = dict(enumerate(parts))
    for mask in masks:
        for r in sorted(rows):
            if r & mask:
                got = swap(rows[r].astype(BHALF), mask)
                rows[r ^ mask] = rows[r ^ mask] + got.astype(FLOAT)
        rows = {r: v for r, v in rows.items() if not r & mask}
    return rows[0]


def srms(values):
    return values * lax.rsqrt(jnp.mean(values * values, axis=-1, keepdims=True) + EPS)


def srms_back(values, gradient):
    scaled = lax.rsqrt(jnp.mean(values * values, axis=-1, keepdims=True) + EPS)
    normed = values * scaled
    return scaled * (gradient - normed * jnp.mean(gradient * normed, axis=-1, keepdims=True))


def swish(values):
    return values * jax.nn.sigmoid(values)


def swish_slope(values):
    sigmoid = jax.nn.sigmoid(values)
    return sigmoid * (1.0 + values * (1.0 - sigmoid))


def angles(position, halves):
    column = jnp.arange(halves, dtype=jnp.int32)
    factor = 1 + jnp.right_shift(jnp.full((halves,), 16384, jnp.int32), column // 4)
    phase = position[:, None] * factor[None, :] % 65536
    turned = phase.astype(jnp.float32) * (2.0 * math.pi / 65536.0)
    return (jnp.cos(turned)[:, None, :], jnp.sin(turned)[:, None, :])


def rotate(values, cosine, sine):
    halves = values.shape[-1] // 2
    first = values[..., :halves]
    second = values[..., halves:]
    return jnp.concatenate(
        [first * cosine - second * sine, first * sine + second * cosine], axis=-1
    )


def unrotate(values, cosine, sine):
    halves = values.shape[-1] // 2
    first = values[..., :halves]
    second = values[..., halves:]
    return jnp.concatenate(
        [first * cosine + second * sine, second * cosine - first * sine], axis=-1
    )


def matmul(left, right):
    return jnp.dot(left, right, preferred_element_type=FLOAT)


def contract_rows(left, right):
    return lax.dot_general(left, right, (((0,), (0,)), ((), ())), preferred_element_type=FLOAT)


def contract_cols(left, right):
    return lax.dot_general(left, right, (((1,), (1,)), ((), ())), preferred_element_type=FLOAT)


def shards(
    tokens,
    query_weight,
    key_weight,
    value_weight,
    modulate_weight,
    output_weight,
    gate_weight,
    linear_weight,
    down_weight,
    cotangent,
    decay_exponent,
):
    tok_count, width = tokens.shape
    heads = decay_exponent.shape[0]
    head_dim = width // heads
    devices = lax.axis_size("seq") * lax.axis_size("tp")
    seq_length = min(SEQ_LEN, tok_count * devices)
    device_place = lax.axis_index("seq") * lax.axis_size("tp") + lax.axis_index("tp")
    first_token = device_place * tok_count
    position = (first_token + jnp.arange(tok_count, dtype=jnp.int32)) % seq_length
    span = seq_length // tok_count
    members = lax.axis_size("tp")
    ring = bits_of(members)
    order = ring[1:] + ring[:1]
    decay_rate = jnp.exp2(-decay_exponent.astype(FLOAT))
    cosine, sine = angles(position, head_dim // 2)
    offsets = jnp.arange(BLOCK, dtype=FLOAT)
    distance = offsets[:, None] - offsets[None, :]
    decay_matrix = jnp.where(
        distance[None] >= 0.0,
        jnp.exp2(-jnp.maximum(distance, 0.0)[None] * decay_rate[:, None, None]),
        0.0,
    )
    query_decay = jnp.exp2(-(offsets + 1.0)[:, None] * decay_rate[None, :])[:, :, None]
    key_decay = jnp.exp2(-(BLOCK - 1.0 - offsets)[:, None] * decay_rate[None, :])[:, :, None]
    block_decay = jnp.exp2(-BLOCK * decay_rate)[:, None, None]
    device_decay = jnp.exp2(-tok_count * decay_rate)
    blocks = tok_count // BLOCK
    inputs = tokens.astype(FLOAT)
    normed = srms(inputs).astype(BHALF)
    pre_query = matmul(normed, query_weight)
    pre_key = matmul(normed, key_weight)
    modulate = matmul(normed, modulate_weight)
    query = rotate(swish(pre_query).reshape(tok_count, heads, head_dim), cosine, sine).astype(BHALF)
    keys = rotate(swish(pre_key).reshape(tok_count, heads, head_dim), cosine, sine).astype(BHALF)
    values = matmul(normed, value_weight).astype(BHALF).reshape(tok_count, heads, head_dim)
    key_states = []
    decayed_queries = []
    decayed_keys = []
    local_state = jnp.zeros((heads, head_dim, head_dim), FLOAT)
    for number in range(blocks):
        window = slice(number * BLOCK, (number + 1) * BLOCK)
        decayed_key = (keys[window].astype(FLOAT) * key_decay).astype(BHALF)
        decayed_query = (query[window].astype(FLOAT) * query_decay).astype(BHALF)
        decayed_keys.append(decayed_key)
        decayed_queries.append(decayed_query)
        contrib = jnp.einsum(
            "jhd,jhe->hde", decayed_key, values[window], preferred_element_type=FLOAT
        )
        key_states.append(contrib)
        local_state = block_decay * local_state + contrib
    state = decayed_scan(local_state, device_decay, span, device_place, False)
    pieces = []
    used_states = []
    for number in range(blocks):
        window = slice(number * BLOCK, (number + 1) * BLOCK)
        block_query = query[window]
        scores = jnp.einsum("ihd,jhd->hij", block_query, keys[window], preferred_element_type=FLOAT)
        probs = (scores * decay_matrix).astype(BHALF)
        intra = jnp.einsum("hij,jhd->ihd", probs, values[window], preferred_element_type=FLOAT)
        state_used = state.astype(BHALF)
        inter = jnp.einsum(
            "ihd,hde->ihe", decayed_queries[number], state_used, preferred_element_type=FLOAT
        )
        used_states.append(state_used)
        state = block_decay * state + key_states[number]
        pieces.append(intra + inter)
    attended = jnp.concatenate(pieces, axis=0).reshape(tok_count, width)
    normed_out = srms(attended)
    gated = (normed_out * modulate).astype(BHALF)
    resid = inputs + matmul(gated, output_weight)
    normed_two = srms(resid).astype(BHALF)
    gathered = jnp.concatenate(gather_group(normed_two, order), axis=0)
    gate_pre = matmul(gathered, gate_weight)
    linear_pre = matmul(gathered, linear_weight)
    hidden = (gate_pre * linear_pre).astype(BHALF)
    feed = scatter_group(
        matmul(hidden, down_weight).reshape(members, tok_count, width), list(reversed(order))
    )
    mixed = (resid + feed).astype(BHALF)
    cot_rows = jnp.concatenate(gather_group(cotangent, order), axis=0)
    down_part = contract_rows(cot_rows, hidden)
    hidden_cot = contract_cols(cot_rows, down_weight)
    gate_back = (hidden_cot * linear_pre).astype(BHALF)
    linear_back = (hidden_cot * gate_pre).astype(BHALF)
    gate_part = contract_rows(gathered, gate_back)
    linear_part = contract_rows(gathered, linear_back)
    normed_parts = contract_cols(gate_back, gate_weight) + contract_cols(linear_back, linear_weight)
    normed_cot = scatter_group(
        normed_parts.reshape(members, tok_count, width), list(reversed(order))
    )
    spread = [members * mask for mask in bits_of(lax.axis_size("seq"))]
    spread = list(reversed(spread))
    gate_grad, linear_grad, down_grad = (
        halve(part.astype(BHALF), spread, device_place).astype(FLOAT)
        for part in (gate_part, linear_part, down_part)
    )
    down_grad = down_grad.T
    resid_cot = cotangent.astype(FLOAT) + srms_back(resid, normed_cot)
    branch_back = resid_cot.astype(BHALF)
    output_part = contract_rows(gated, branch_back)
    gated_cot = contract_cols(branch_back, output_weight)
    modulate_back = (gated_cot * normed_out).astype(BHALF)
    attended_back = (
        srms_back(attended, gated_cot * modulate).astype(BHALF).reshape(tok_count, heads, head_dim)
    )
    direct = []
    for number in range(blocks):
        window = slice(number * BLOCK, (number + 1) * BLOCK)
        direct.append(
            jnp.einsum(
                "ihd,ihe->hde",
                decayed_queries[number],
                attended_back[window],
                preferred_element_type=FLOAT,
            )
        )
    inbound = jnp.zeros_like(local_state)
    for number in reversed(range(blocks)):
        inbound = block_decay * inbound + direct[number]
    outer = decayed_scan(inbound, device_decay, span, device_place, True)
    accum = jnp.zeros_like(local_state)
    query_parts = []
    key_parts = []
    value_parts = []
    for number in reversed(range(blocks)):
        window = slice(number * BLOCK, (number + 1) * BLOCK)
        state_cot = outer + accum
        outer = block_decay * outer
        accum = block_decay * accum + direct[number]
        block_query = query[window]
        block_key = keys[window]
        block_value = values[window]
        block_back = attended_back[window]
        key_part = (
            jnp.einsum("hde,jhe->jhd", state_cot.astype(BHALF), block_value, preferred_element_type=FLOAT)
            * key_decay
        )
        value_part = jnp.einsum(
            "jhd,hde->jhe", decayed_keys[number], state_cot.astype(BHALF), preferred_element_type=FLOAT
        )
        scores = jnp.einsum("ihd,jhd->hij", block_query, block_key, preferred_element_type=FLOAT)
        probs = (scores * decay_matrix).astype(BHALF)
        prob_cot = jnp.einsum("ihe,jhe->hij", block_back, block_value, preferred_element_type=FLOAT)
        score_back = (prob_cot * decay_matrix).astype(BHALF)
        value_part = value_part + jnp.einsum(
            "hij,ihe->jhe", probs, block_back, preferred_element_type=FLOAT
        )
        key_part = key_part + jnp.einsum(
            "hij,ihd->jhd", score_back, block_query, preferred_element_type=FLOAT
        )
        query_part = jnp.einsum("hij,jhd->ihd", score_back, block_key, preferred_element_type=FLOAT)
        query_part = (
            query_part
            + jnp.einsum(
                "ihe,hde->ihd", block_back, used_states[number], preferred_element_type=FLOAT
            )
            * query_decay
        )
        query_parts.insert(0, query_part)
        key_parts.insert(0, key_part)
        value_parts.insert(0, value_part)
    query_cot = jnp.concatenate(query_parts, axis=0)
    key_cot = jnp.concatenate(key_parts, axis=0)
    value_cot = jnp.concatenate(value_parts, axis=0)
    query_back = (
        unrotate(query_cot, cosine, sine).reshape(tok_count, width) * swish_slope(pre_query)
    ).astype(BHALF)
    key_back = (
        unrotate(key_cot, cosine, sine).reshape(tok_count, width) * swish_slope(pre_key)
    ).astype(BHALF)
    value_back = value_cot.reshape(tok_count, width).astype(BHALF)
    normed_grad = contract_cols(query_back, query_weight) + contract_cols(key_back, key_weight)
    normed_grad = (
        normed_grad
        + contract_cols(value_back, value_weight)
        + contract_cols(modulate_back, modulate_weight)
    )
    tokens_grad = resid_cot + srms_back(inputs, normed_grad)
    everyone = bits_of(devices)
    rest = everyone[1:]
    across = members // 2
    lines = [[m for m in rest if m < members], [m for m in rest if members <= m < members * across],
             [m for m in rest if m >= members * across]]
    def turn(k):
        return [1] + [m for i in range(3) for m in lines[(i + k) % 3]]
    query_grad, key_grad, value_grad, modulate_grad, output_grad = (
        all_reduce(part.astype(BHALF), turn(k), device_place)
        for k, part in enumerate((
            contract_rows(normed, query_back),
            contract_rows(normed, key_back),
            contract_rows(normed, value_back),
            contract_rows(normed, modulate_back),
            output_part,
        ))
    )
    return (
        mixed,
        tokens_grad,
        query_grad,
        key_grad,
        value_grad,
        modulate_grad,
        output_grad,
        gate_grad,
        linear_grad,
        down_grad,
    )


def solution(mesh):
    return jax.shard_map(
        shards,
        mesh=mesh,
        in_specs=(
            P(("seq", "tp"), None),
            P(),
            P(),
            P(),
            P(),
            P(),
            P(None, "tp"),
            P(None, "tp"),
            P("tp", None),
            P(("seq", "tp"), None),
            P(),
        ),
        out_specs=(
            P(("seq", "tp"), None),
            P(("seq", "tp"), None),
            P(),
            P(),
            P(),
            P(),
            P(),
            P("seq", "tp"),
            P("seq", "tp"),
            P("tp", "seq"),
        ),
        check_vma=False,
    )
```

```python
import functools
import math

import jax
import jax.numpy as jnp
from jax import lax
from jax.experimental import pallas as pl
from jax.experimental.pallas import tpu as pltpu
from jax.sharding import PartitionSpec as P

BLOCK = 256
SEQ_LEN = 16384
EPS = 1e-06
FLOAT = jnp.float32
BHALF = jnp.bfloat16
VMEM_BYTES = 60 * 1024 * 1024


def bits_of(count):
    return [1 << b for b in range(count.bit_length() - 1)]


def swap(value, mask, axes=("seq", "tp")):
    count = lax.axis_size(axes)
    return lax.ppermute(value, axes, [(s, s ^ mask) for s in range(count)])


def bit_of(place, mask):
    return (place // mask) % 2


def after(value, *others):
    return lax.optimization_barrier((value,) + others)[0]


def halve(value, masks, place):
    for mask in masks:
        halves = value.reshape((2, value.shape[0] // 2) + value.shape[1:])
        bit = bit_of(place, mask)
        keep = lax.dynamic_index_in_dim(halves, bit, 0, False)
        send = lax.dynamic_index_in_dim(halves, 1 - bit, 0, False)
        value = (keep.astype(FLOAT) + swap(send, mask).astype(FLOAT)).astype(BHALF)
    return value


def double(value, masks, place):
    for mask in masks:
        other = swap(value, mask)
        bit = bit_of(place, mask)
        first = jnp.where(bit == 0, value, other)
        second = jnp.where(bit == 0, other, value)
        value = jnp.concatenate([first, second], axis=0)
    return value


def fold(value, masks):
    for mask in masks:
        half = value.shape[0] // 2
        got = swap(value[half:], mask)
        value = (value[:half].astype(FLOAT) + got.astype(FLOAT)).astype(BHALF)
    return value[0]


def decayed_scan(state, rate, unit, span, place, reverse):
    heads = state.shape[0]
    half = heads // 2
    bit = bit_of(place, 1)
    halves = state.reshape((2, half) + state.shape[1:])
    mine = lax.dynamic_index_in_dim(halves, bit, 0, False)
    theirs = lax.dynamic_index_in_dim(halves, 1 - bit, 0, False)
    other = swap(theirs.astype(BHALF), 1).astype(FLOAT)
    own_rate = lax.dynamic_index_in_dim(rate.reshape(2, half), bit, 0, False)

    def power(count):
        return jnp.exp2(-unit * count * own_rate)[:, None, None]

    later = 1 - bit if reverse else bit
    core_later = jnp.where(later == 1, mine, other)
    core_first = jnp.where(later == 1, other, mine)
    total = power(1.0) * core_first + core_later
    prefix = jnp.zeros_like(total)
    mark = None
    for mask in bits_of(span)[1:]:
        bit = bit_of(place, mask)
        later = 1 - bit if reverse else bit
        sent = swap(total.astype(BHALF), mask)
        mark = sent if mark is None else mark
        got = sent.astype(FLOAT)
        within = (place % mask) // 2
        if reverse:
            within = mask // 2 - 1 - within
        scale = power(2.0 * within.astype(FLOAT))
        prefix = prefix + jnp.where(later == 1, scale * got, 0.0)
        low = jnp.where(later == 1, got, total)
        high = jnp.where(later == 1, total, got)
        total = power(float(mask)) * low + high
    second_pre = power(1.0) * prefix + core_first
    bit = bit_of(place, 1)
    later = 1 - bit if reverse else bit
    own = jnp.where(later == 1, second_pre, prefix)
    away = jnp.where(later == 1, prefix, second_pre)
    got = swap(away.astype(BHALF), 1).astype(FLOAT)
    first = jnp.where(bit == 0, own, got)
    second = jnp.where(bit == 0, got, own)
    return jnp.concatenate([first, second], axis=0), mark


def gather_group(value, masks):
    rows = {0: value}
    for mask in masks:
        for r in list(rows):
            rows[r | mask] = swap(rows[r], mask)
    return [rows[r] for r in range(len(rows))]


def dot_nn(left, right):
    return jnp.dot(left, right, preferred_element_type=FLOAT)


def dot_tn(left, right):
    return lax.dot_general(left, right, (((0,), (0,)), ((), ())), preferred_element_type=FLOAT)


def dot_nt(left, right):
    return lax.dot_general(left, right, (((1,), (1,)), ((), ())), preferred_element_type=FLOAT)


def srms(values):
    return values * lax.rsqrt(jnp.mean(values * values, axis=-1, keepdims=True) + EPS)


def srms_back(values, gradient):
    scaled = lax.rsqrt(jnp.mean(values * values, axis=-1, keepdims=True) + EPS)
    normed = values * scaled
    return scaled * (gradient - normed * jnp.mean(gradient * normed, axis=-1, keepdims=True))


def swish(values):
    return values * jax.nn.sigmoid(values)


def swish_slope(values):
    sigmoid = jax.nn.sigmoid(values)
    return sigmoid * (1.0 + values * (1.0 - sigmoid))


def half_turn(values):
    return pltpu.roll(values, values.shape[-1] // 2, 1)


def rotate(values, cosine, sine):
    return values * cosine + half_turn(values) * sine


def unrotate(values, cosine, sine):
    return values * cosine - half_turn(values) * sine


def row_decay(rate, size, start, sign):
    offset = lax.broadcasted_iota(jnp.int32, (BLOCK, size), 0).astype(FLOAT)
    return jnp.exp2(-(start + sign * offset) * rate)


def query_decay(rate, size):
    return row_decay(rate, size, 1.0, 1.0)


def key_decay(rate, size):
    return row_decay(rate, size, BLOCK - 1.0, -1.0)


def decay_matrix(rate):
    row = lax.broadcasted_iota(jnp.int32, (BLOCK, BLOCK), 0)
    column = lax.broadcasted_iota(jnp.int32, (BLOCK, BLOCK), 1)
    distance = (row - column).astype(FLOAT)
    return jnp.where(distance >= 0.0, jnp.exp2(-jnp.maximum(distance, 0.0) * rate), 0.0)


def scaled_by(factor_exponent, values):
    return jnp.exp2(jnp.full(values.shape, factor_exponent, FLOAT)) * values


def shape_of(shape, dtype):
    return jax.ShapeDtypeStruct(shape, dtype)


SMEM_SPEC = pl.BlockSpec(memory_space=pltpu.SMEM)


def call(body, grid, in_specs, out_specs, out_shape, flops, moved, scratch=()):
    return pl.pallas_call(
        body,
        grid=grid,
        in_specs=in_specs,
        out_specs=out_specs,
        out_shape=out_shape,
        scratch_shapes=scratch,
        cost_estimate=pl.CostEstimate(flops=flops, bytes_accessed=moved, transcendentals=0),
        compiler_params=pltpu.CompilerParams(vmem_limit_bytes=VMEM_BYTES),
    )


def kv_body(heads, rate, x, wk, wv, cosine, sine, normed, pre_key, keys, values, contrib, local):
    step = pl.program_id(0)
    size = cosine.shape[1]
    blocks = x.shape[0] // BLOCK

    @pl.when(step == 0)
    def _():
        normed[...] = srms(x[...].astype(FLOAT)).astype(BHALF)

    rows = normed[...]
    pre = dot_nn(rows, wk[...])
    pre_key[...] = pre
    val = dot_nn(rows, wv[...]).astype(BHALF)
    values[...] = val
    for h in range(heads):
        part = slice(h * size, (h + 1) * size)
        own_rate = rate[step * heads + h]
        key = rotate(swish(pre[:, part]), cosine[...], sine[...]).astype(BHALF)
        keys[:, part] = key
        decay = key_decay(own_rate, size)
        total = None
        for b in range(blocks):
            span = slice(b * BLOCK, (b + 1) * BLOCK)
            decayed = (key[span].astype(FLOAT) * decay).astype(BHALF)
            state = dot_tn(decayed, val[span, part])
            contrib[b, h] = state
            total = state if total is None else scaled_by(-BLOCK * own_rate, total) + state
        local[h] = total


def kv(rate, x, wk, wv, cosine, sine, steps):
    tokens, width = x.shape
    heads = rate.shape[0]
    size = width // heads
    group = heads // steps
    cols = group * size
    blocks = tokens // BLOCK
    tile = lambda n: pl.BlockSpec((n, cols), lambda i: (0, i))
    whole = lambda a: pl.BlockSpec(a.shape, lambda i: (0, 0))
    return call(
        functools.partial(kv_body, group),
        (steps,),
        [SMEM_SPEC, whole(x), tile(width), tile(width), whole(cosine), whole(sine)],
        [
            whole(x),
            tile(tokens),
            tile(tokens),
            tile(tokens),
            pl.BlockSpec((blocks, group, size, size), lambda i: (0, i, 0, 0)),
            pl.BlockSpec((group, size, size), lambda i: (i, 0, 0)),
        ],
        [
            shape_of(x.shape, BHALF),
            shape_of(x.shape, FLOAT),
            shape_of(x.shape, BHALF),
            shape_of(x.shape, BHALF),
            shape_of((blocks, heads, size, size), FLOAT),
            shape_of((heads, size, size), FLOAT),
        ],
        4 * tokens * width * width,
        12 * tokens * width + 4 * width * width,
    )(rate, x, wk, wv, cosine, sine)


def qu_body(heads, rate, rows, wq, wu, cosine, sine, keys, values, pre_query, query, gate, intra):
    step = pl.program_id(0)
    size = cosine.shape[1]
    blocks = rows.shape[0] // BLOCK
    pre = dot_nn(rows[...], wq[...])
    pre_query[...] = pre
    gate[...] = dot_nn(rows[...], wu[...])
    for h in range(heads):
        part = slice(h * size, (h + 1) * size)
        q = rotate(swish(pre[:, part]), cosine[...], sine[...]).astype(BHALF)
        query[:, part] = q
        decay = decay_matrix(rate[step * heads + h])
        for b in range(blocks):
            span = slice(b * BLOCK, (b + 1) * BLOCK)
            weights = (dot_nt(q[span], keys[span, part]) * decay).astype(BHALF)
            intra[span, part] = dot_nn(weights, values[span, part])


def qu(rate, rows, wq, wu, cosine, sine, keys, values, steps):
    tokens, width = rows.shape
    heads = rate.shape[0]
    group = heads // steps
    cols = group * (width // heads)
    tile = lambda n: pl.BlockSpec((n, cols), lambda i: (0, i))
    whole = lambda a: pl.BlockSpec(a.shape, lambda i: (0, 0))
    return call(
        functools.partial(qu_body, group),
        (steps,),
        [SMEM_SPEC, whole(rows), tile(width), tile(width), whole(cosine), whole(sine)]
        + [tile(tokens)] * 2,
        [tile(tokens)] * 4,
        [shape_of(rows.shape, d) for d in (FLOAT, BHALF, FLOAT, FLOAT)],
        4 * tokens * width * width,
        20 * tokens * width + 4 * width * width,
    )(rate, rows, wq, wu, cosine, sine, keys, values)


def join_body(heads, use_next, rate, x, intra, query, gate, state, before, wo, *outs):
    attended, gated, resid, normed, used = outs
    size = state.shape[1]
    pieces = []
    for h in range(heads):
        part = slice(h * size, (h + 1) * size)
        own_rate = rate[h]
        here = state[h]
        if use_next:
            here = scaled_by(-BLOCK * own_rate, here) + before[h]
        here = here.astype(BHALF)
        used[h] = here
        q = (query[:, part].astype(FLOAT) * query_decay(own_rate, size)).astype(BHALF)
        pieces.append(intra[:, part] + dot_nn(q, here))
    full = jnp.concatenate(pieces, axis=1)
    attended[...] = full
    g = (srms(full) * gate[...]).astype(BHALF)
    gated[...] = g
    r = x[...].astype(FLOAT) + dot_nn(g, wo[...])
    resid[...] = r
    normed[...] = srms(r).astype(BHALF)


def join(block, rate, x, intra, query, gate, state, contrib, wo):
    width = x.shape[1]
    heads, size = state.shape[0], state.shape[1]
    before = contrib
    if block > 1:
        for b in range(block - 1):
            state = jnp.exp2(-BLOCK * rate)[:, None, None] * state + contrib[b]
    row = pl.BlockSpec((BLOCK, width), lambda i: (block, 0))
    out_row = pl.BlockSpec((BLOCK, width), lambda i: (0, 0))
    cube = pl.BlockSpec((heads, size, size), lambda i: (0, 0, 0))
    earlier = max(block - 1, 0)
    return call(
        functools.partial(join_body, heads, block > 0),
        (1,),
        [SMEM_SPEC, row, row, row, row, cube]
        + [pl.BlockSpec((None, heads, size, size), lambda i: (earlier, 0, 0, 0))]
        + [pl.BlockSpec(wo.shape, lambda i: (0, 0))],
        [out_row] * 4 + [cube],
        [shape_of((BLOCK, width), d) for d in (FLOAT, BHALF, FLOAT, BHALF)]
        + [shape_of((heads, size, size), BHALF)],
        2 * BLOCK * width * (width + size),
        24 * BLOCK * width + 2 * width * width,
    )(rate, x, intra, query, gate, state, before, wo)


def unit_body(n0, n1, c0, c1, gate_t, linear_t, down, keep, ship, hidden, gate_back, linear_back):
    rows = jnp.concatenate([n0[...], n1[...]], axis=0)
    cots = jnp.concatenate([c0[...], c1[...]], axis=0)
    gate = dot_nt(rows, gate_t[...])
    linear = dot_nt(rows, linear_t[...])
    inner = (gate * linear).astype(BHALF)
    hidden[...] = inner
    inner_cot = dot_nt(cots, down[...])
    gb = (inner_cot * linear).astype(BHALF)
    lb = (inner_cot * gate).astype(BHALF)
    gate_back[...] = gb
    linear_back[...] = lb
    feed = dot_nn(inner, down[...])
    cot = dot_nn(gb, gate_t[...]) + dot_nn(lb, linear_t[...])
    keep[0] = cot[:BLOCK]
    keep[1] = feed[:BLOCK]
    ship[0] = cot[BLOCK:].astype(BHALF)
    ship[1] = feed[BLOCK:].astype(BHALF)


def unit(block, rows, cots, gate_t, linear_t, down):
    width = rows[0].shape[1]
    inner = down.shape[0]
    piece = pl.BlockSpec((BLOCK, width), lambda i: (0, 0))
    cot = pl.BlockSpec((BLOCK, width), lambda i: (block, 0))
    whole = lambda s: pl.BlockSpec(s, lambda i: (0,) * len(s))
    wide = (2 * BLOCK, inner)
    pair = (2, BLOCK, width)
    return call(
        unit_body,
        (1,),
        [piece] * 2 + [cot] * 2 + [whole(down.shape)] * 3,
        [whole(pair)] * 2 + [whole(wide)] * 3,
        [shape_of(pair, FLOAT), shape_of(pair, BHALF)] + [shape_of(wide, BHALF)] * 3,
        24 * BLOCK * width * inner,
        6 * width * inner + 20 * BLOCK * width,
    )(*rows, *cots, gate_t, linear_t, down)


def place_in(order, count, shard, place):
    relative = jnp.bitwise_xor(shard, place)
    position = 0
    for mask in order:
        position = position * 2 + jnp.bitwise_and(relative // mask, 1)
    return position


def unit_grads_body(groups, orders, place, *refs):
    per = 2 + 2 + 3
    ins = refs[: groups * per]
    pair_out, down_out = refs[groups * per : groups * per + 2]
    rows, cots, hidden, gate_back, linear_back, sems = refs[groups * per + 2 :]
    copies = [[] for _ in range(groups)]
    for g in range(groups):
        n0, n1, c0, c1, h, gb, lb = ins[g * per : (g + 1) * per]
        block = g % 2
        span = pl.ds(block * BLOCK, BLOCK)
        moves = [
            (gb, gate_back.at[g]),
            (n0, rows.at[g, pl.ds(0, BLOCK)]),
            (n1, rows.at[g, pl.ds(BLOCK, BLOCK)]),
            (lb, linear_back.at[g]),
            (h, hidden.at[g]),
            (c0.at[span], cots.at[g, pl.ds(0, BLOCK)]),
            (c1.at[span], cots.at[g, pl.ds(BLOCK, BLOCK)]),
        ]
        for k, (source, target) in enumerate(moves):
            copies[g].append(pltpu.make_async_copy(source, target, sems.at[g, k]))
    for first, last in ((0, 3), (3, 4), (4, 7)):
        for g in range(groups):
            for copy in copies[g][first:last]:
                copy.start()
    count = pair_out.shape[0]
    here = place[0]

    def total(left, right, first, last):
        acc = None
        for g in range(groups):
            for copy in copies[g][first:last]:
                copy.wait()
            term = dot_tn(left[g], right[g])
            acc = term if acc is None else acc + term
        return acc

    def store(acc, put, order):
        size = acc.shape[1] // count
        for shard in range(count):
            put(place_in(order, count, shard, here), acc[:, shard * size : (shard + 1) * size])

    def put_pair(k):
        def put(position, value):
            pair_out[position, k] = value.astype(BHALF)
        return put

    def put_down(position, value):
        down_out[position] = value.astype(BHALF)

    store(total(gate_back, rows, 0, 3), put_pair(0), orders[0])
    store(total(linear_back, rows, 3, 4), put_pair(1), orders[0])
    store(total(hidden, cots, 4, 7), put_down, orders[1])


def unit_grads(place, groups, orders, count):
    inner = groups[0][4].shape[1]
    width = groups[0][0].shape[1]
    flat = [a for group in groups for a in group]
    any_spec = pl.BlockSpec(memory_space=pl.ANY)
    size = width // count
    pair = (count, 2, inner, size)
    single = (count, inner, size)
    n = len(groups)
    whole = lambda s: pl.BlockSpec(s, lambda i: (0,) * len(s))
    return call(
        functools.partial(unit_grads_body, n, orders),
        (1,),
        [SMEM_SPEC] + [any_spec] * len(flat),
        [whole(pair), whole(single)],
        [shape_of(pair, BHALF), shape_of(single, BHALF)],
        12 * n * BLOCK * width * inner,
        n * 2 * BLOCK * (4 * width + 6 * inner) + 6 * width * inner,
        scratch=[
            pltpu.VMEM((n, 2 * BLOCK, width), BHALF),
            pltpu.VMEM((n, 2 * BLOCK, width), BHALF),
            pltpu.VMEM((n, 2 * BLOCK, inner), BHALF),
            pltpu.VMEM((n, 2 * BLOCK, inner), BHALF),
            pltpu.VMEM((n, 2 * BLOCK, inner), BHALF),
            pltpu.SemaphoreType.DMA((n, 7)),
        ],
    )(place, *flat)


def turn_body(heads, rate, keep, got, far, resid, cot, attended, gate, query, wo, *outs):
    resid_cot, branch, modulate, back, direct = outs
    size = direct.shape[1]
    normed_cot = keep[0] + got[0].astype(FLOAT)
    for k in range(far.shape[0]):
        normed_cot = normed_cot + far[k].astype(FLOAT)
    rc = cot[...].astype(FLOAT) + srms_back(resid[...], normed_cot)
    resid_cot[...] = rc
    bb = rc.astype(BHALF)
    branch[...] = bb
    gated_cot = dot_nt(bb, wo[...])
    att = attended[...]
    modulate[...] = (gated_cot * srms(att)).astype(BHALF)
    ab = srms_back(att, gated_cot * gate[...]).astype(BHALF)
    back[...] = ab
    for h in range(heads):
        part = slice(h * size, (h + 1) * size)
        q = (query[:, part].astype(FLOAT) * query_decay(rate[h], size)).astype(BHALF)
        direct[h] = dot_tn(q, ab[:, part])


def turn(block, rate, keep, got, far, resid, cot, attended, gate, query, wo):
    width = resid.shape[1]
    heads = rate.shape[0]
    size = width // heads
    row = pl.BlockSpec((BLOCK, width), lambda i: (block, 0))
    own = pl.BlockSpec((BLOCK, width), lambda i: (0, 0))
    first = pl.BlockSpec((1, BLOCK, width), lambda i: (0, 0, 0))
    cube = pl.BlockSpec((heads, size, size), lambda i: (0, 0, 0))
    return call(
        functools.partial(turn_body, heads),
        (1,),
        [SMEM_SPEC, first, first, pl.BlockSpec(far.shape, lambda i: (0, 0, 0)), own, row, own]
        + [row, row, pl.BlockSpec(wo.shape, lambda i: (0, 0))],
        [own] * 4 + [cube],
        [shape_of((BLOCK, width), d) for d in (FLOAT, BHALF, BHALF, BHALF)]
        + [shape_of((heads, size, size), FLOAT)],
        2 * BLOCK * width * (width + size),
        32 * BLOCK * width + 2 * width * width,
    )(rate, keep, got, far, resid, cot, attended, gate, query, wo)


def query_body(heads, blocks, rate, pre_query, query, keys, values, cosine, sine, *refs):
    backs = refs[:blocks]
    used = refs[blocks : 2 * blocks]
    query_back, key_part, value_part = refs[2 * blocks :]
    step = pl.program_id(0)
    size = cosine.shape[1]
    for h in range(heads):
        part = slice(h * size, (h + 1) * size)
        own_rate = rate[step * heads + h]
        decay = decay_matrix(own_rate)
        row = query_decay(own_rate, size)
        for b in range(blocks):
            span = slice(b * BLOCK, (b + 1) * BLOCK)
            q, k, v = query[span, part], keys[span, part], values[span, part]
            ab = backs[b][:, part]
            weights = (dot_nt(q, k) * decay).astype(BHALF)
            weights_back = (dot_nt(ab, v) * decay).astype(BHALF)
            value_part[span, part] = dot_tn(weights, ab)
            key_part[span, part] = dot_tn(weights_back, q)
            cot = dot_nn(weights_back, k) + row * dot_nt(ab, used[b][h])
            cot = unrotate(cot, cosine[span], sine[span])
            query_back[span, part] = (cot * swish_slope(pre_query[span, part])).astype(BHALF)


def query_side(rate, pre_query, query, keys, values, cosine, sine, backs, used, steps):
    tokens, width = query.shape
    heads = rate.shape[0]
    size = width // heads
    group = heads // steps
    cols = group * size
    blocks = len(backs)
    tile = pl.BlockSpec((tokens, cols), lambda i: (0, i))
    whole = lambda a: pl.BlockSpec(a.shape, lambda i: (0, 0))
    return call(
        functools.partial(query_body, group, blocks),
        (steps,),
        [SMEM_SPEC] + [tile] * 4 + [whole(cosine), whole(sine)]
        + [pl.BlockSpec((BLOCK, cols), lambda i: (0, i))] * blocks
        + [pl.BlockSpec((group, size, size), lambda i: (i, 0, 0))] * blocks,
        [tile] * 3,
        [shape_of(query.shape, d) for d in (BHALF, FLOAT, FLOAT)],
        12 * tokens * width * BLOCK,
        24 * tokens * width,
    )(rate, pre_query, query, keys, values, cosine, sine, *backs, *used)


def key_body(heads, blocks, rate, pre_key, keys, values, key_part, value_part, *refs):
    cosine, sine, state = refs[:3]
    direct = refs[3 : 3 + blocks]
    key_back, value_back = refs[3 + blocks :]
    step = pl.program_id(0)
    size = cosine.shape[1]
    for h in range(heads):
        part = slice(h * size, (h + 1) * size)
        own_rate = rate[step * heads + h]
        decay = key_decay(own_rate, size)
        here = state[h]
        for b in reversed(range(blocks)):
            span = slice(b * BLOCK, (b + 1) * BLOCK)
            used = here.astype(BHALF)
            cot = key_part[span, part] + decay * dot_nt(values[span, part], used)
            decayed = (keys[span, part].astype(FLOAT) * decay).astype(BHALF)
            vcot = value_part[span, part] + dot_nn(decayed, used)
            cot = unrotate(cot, cosine[span], sine[span])
            key_back[span, part] = (cot * swish_slope(pre_key[span, part])).astype(BHALF)
            value_back[span, part] = vcot.astype(BHALF)
            if b:
                here = scaled_by(-BLOCK * own_rate, here) + direct[b][h]


def key_side(rate, pre_key, keys, values, key_part, value_part, cosine, sine, state, direct, steps):
    tokens, width = keys.shape
    heads = rate.shape[0]
    size = width // heads
    group = heads // steps
    cols = group * size
    blocks = len(direct)
    tile = pl.BlockSpec((tokens, cols), lambda i: (0, i))
    whole = lambda a: pl.BlockSpec(a.shape, lambda i: (0, 0))
    cube = pl.BlockSpec((group, size, size), lambda i: (i, 0, 0))
    return call(
        functools.partial(key_body, group, blocks),
        (steps,),
        [SMEM_SPEC] + [tile] * 5 + [whole(cosine), whole(sine), cube] + [cube] * blocks,
        [tile] * 2,
        [shape_of(keys.shape, BHALF)] * 2,
        4 * tokens * width * size,
        20 * tokens * width,
    )(rate, pre_key, keys, values, key_part, value_part, cosine, sine, state, *direct)


def grads_body(lefts, pairs, core, *refs):
    left = refs[:lefts]
    right = refs[lefts:-1]
    out = refs[-1]
    for k, (l, rs) in enumerate(pairs):
        acc = None
        start = 0
        for piece in rs:
            r = right[piece]
            rows = r.shape[0]
            term = dot_tn(left[l][start : start + rows], r[...])
            start += rows
            acc = term if acc is None else acc + term
        out[0, k] = acc.astype(BHALF)


def grads(core, lefts, rights, pairs):
    tokens, width = lefts[0].shape
    cols = rights[0].shape[1]
    half = width // 2
    spec = pltpu.PrefetchScalarGridSpec(
        num_scalar_prefetch=1,
        grid=(2,),
        in_specs=[pl.BlockSpec((tokens, half), lambda i, c: (0, i ^ c[0]))] * len(lefts)
        + [pl.BlockSpec(r.shape, lambda i, c: (0, 0)) for r in rights],
        out_specs=pl.BlockSpec((1, len(pairs), half, cols), lambda i, c: (i, 0, 0, 0)),
    )
    n = len(pairs)
    body = functools.partial(grads_body, len(lefts), pairs)
    return pl.pallas_call(
        body,
        grid_spec=spec,
        out_shape=shape_of((2, n, half, cols), BHALF),
        cost_estimate=pl.CostEstimate(
            flops=2 * n * tokens * width * cols, bytes_accessed=4 * n * width * cols, transcendentals=0
        ),
        compiler_params=pltpu.CompilerParams(vmem_limit_bytes=VMEM_BYTES),
    )(core, *lefts, *rights)


def tokens_body(x, rc, qb, kb, vb, mb, wq, wk, wv, wm, out):
    grad = dot_nt(qb[...], wq[...]) + dot_nt(kb[...], wk[...])
    grad = grad + dot_nt(vb[...], wv[...]) + dot_nt(mb[...], wm[...])
    out[...] = rc[...] + srms_back(x[...].astype(FLOAT), grad)


def tokens_side(block, x, rc, qb, kb, vb, mb, weights):
    tokens, width = x.shape
    row = pl.BlockSpec((BLOCK, width), lambda i: (block, 0))
    own = pl.BlockSpec((BLOCK, width), lambda i: (0, 0))
    whole = pl.BlockSpec((width, width), lambda i: (0, 0))
    return call(
        tokens_body,
        (1,),
        [row, own, row, row, row, own] + [whole] * 4,
        own,
        shape_of((BLOCK, width), FLOAT),
        8 * BLOCK * width * width,
        8 * width * width + 20 * BLOCK * width,
    )(x, rc, qb, kb, vb, mb, *weights)


def angle_tables(position, halves):
    column = jnp.arange(halves, dtype=jnp.int32)
    factor = 1 + jnp.right_shift(jnp.full((halves,), 16384, jnp.int32), column // 4)
    phase = position[:, None] * factor[None, :] % 65536
    turned = phase.astype(FLOAT) * (2.0 * math.pi / 65536.0)
    cosine, sine = jnp.cos(turned), jnp.sin(turned)
    return jnp.concatenate([cosine, cosine], 1), jnp.concatenate([-sine, sine], 1)


def shards(
    tokens,
    query_weight,
    key_weight,
    value_weight,
    modulate_weight,
    output_weight,
    gate_weight,
    linear_weight,
    down_weight,
    cotangent,
    decay_exponent,
):
    count, width = tokens.shape
    heads = decay_exponent.shape[0]
    size = width // heads
    runs, members = lax.axis_size("seq"), lax.axis_size("tp")
    devices = runs * members
    length = min(SEQ_LEN, count * devices)
    span = length // count
    blocks = count // BLOCK
    seq_place = lax.axis_index("seq")
    place = seq_place * members + lax.axis_index("tp")
    core = bit_of(place, 1).astype(jnp.int32).reshape(1)
    position = (place * count + jnp.arange(count, dtype=jnp.int32)) % length
    rate = jnp.exp2(-decay_exponent.astype(FLOAT))
    cosine, sine = angle_tables(position, size // 2)
    ring = bits_of(members)
    far = ring[1:]

    normed, pre_key, keys, values, contrib, local = kv(
        rate, tokens, key_weight, value_weight, cosine, sine, 2
    )
    state, mark = decayed_scan(local, rate, float(count), span, place, False)
    pre_query, query, gate, intra = qu(
        rate, normed, query_weight, modulate_weight, cosine, sine, keys, values, 2
    )
    cots = gather_group(after(cotangent, mark), far + [1])
    joined = [
        join(b, rate, tokens, intra, query, gate, state, contrib, output_weight)
        for b in range(blocks)
    ]

    gate_t, linear_t = gate_weight.T, linear_weight.T
    gathered = [gather_group(joined[b][3], far + [1]) for b in range(blocks)]
    results = {}
    for r in range(0, members, 2):
        for b in range(blocks):
            results[r, b] = unit(
                b, gathered[b][r : r + 2], cots[r : r + 2], gate_t, linear_t, down_weight
            )
    groups = [
        tuple(gathered[b][r : r + 2]) + tuple(cots[r : r + 2]) + tuple(results[r, b][2:])
        for r in range(0, members, 2)
        for b in range(blocks)
    ]
    near = {}
    for key, value in results.items():
        near[key] = (value[0], swap(value[1], 1))
    arrived = {}
    for part in range(2):
        for b in range(blocks):
            rows = {
                r: near[r, b][0][part] + near[r, b][1][part].astype(FLOAT)
                for r in range(2, members, 2)
            }
            got = []
            for mask in reversed(far):
                for r in [r for r in rows if r & mask]:
                    value = swap(rows.pop(r).astype(BHALF), mask)
                    if r == mask:
                        got.append(value)
                    else:
                        rows[r ^ mask] = rows[r ^ mask] + value.astype(FLOAT)
            arrived[b, part] = got

    turned = [
        turn(
            b, rate, near[0, b][0], near[0, b][1], jnp.stack(arrived[b, 0]), joined[b][2],
            cotangent, joined[b][0], gate, query, output_weight,
        )
        for b in range(blocks)
    ]
    line = bits_of(runs)
    across = max(members // 2, 1)
    orders = (line, [m for m in line if m >= across] + [m for m in line if m < across])
    seq_scalar = seq_place.astype(jnp.int32).reshape(1)
    pair_part, down_part = unit_grads(seq_scalar, groups, orders, runs)

    decays = jnp.exp2(-BLOCK * rate)[:, None, None]
    inbound = turned[blocks - 1][4]
    for b in reversed(range(blocks - 1)):
        inbound = decays * inbound + turned[b][4]
    outer, _ = decayed_scan(inbound, rate, float(count), span, place, True)
    backs = [t[3] for t in turned]
    query_back, key_part, value_part = query_side(
        rate, pre_query, query, keys, values, cosine, sine, backs, [j[4] for j in joined], 2
    )
    gated = jnp.concatenate([j[1] for j in joined], axis=0)
    early = grads(
        core,
        [gated, normed],
        [t[1] for t in turned] + [t[2] for t in turned] + [query_back],
        [
            (0, list(range(blocks))),
            (1, list(range(blocks, 2 * blocks))),
            (1, [2 * blocks]),
        ],
    )
    key_back, value_back = key_side(
        rate, pre_key, keys, values, key_part, value_part, cosine, sine, outer,
        [t[4] for t in turned], 2,
    )
    late = grads(core, [normed], [key_back, value_back], [(0, [0]), (0, [1])])
    weights = (query_weight, key_weight, value_weight, modulate_weight)
    tokens_grad = jnp.concatenate(
        [
            tokens_side(
                b, tokens, turned[b][0], query_back, key_back, value_back, turned[b][2], weights
            )
            for b in range(blocks)
        ],
        axis=0,
    )

    mixed = jnp.concatenate(
        [
            (
                joined[b][2] + near[0, b][0][1] + near[0, b][1][1].astype(FLOAT)
                + sum(a.astype(FLOAT) for a in arrived[b, 1])
            ).astype(BHALF)
            for b in range(blocks)
        ],
        axis=0,
    )
    masks = [[members * m for m in order] for order in orders]
    pair_grad = fold(pair_part, masks[0]).astype(FLOAT)
    down_grad = fold(down_part, masks[1]).astype(FLOAT)
    gate_grad, linear_grad = pair_grad[0].T, pair_grad[1].T

    rest = bits_of(devices)[1:]
    lines = [
        [m for m in rest if m < members],
        [m for m in rest if members <= m < members * across],
        [m for m in rest if m >= members * across],
    ]

    def reduced(part):
        kept = (part[0].astype(FLOAT) + swap(part[1], 1).astype(FLOAT)).astype(BHALF)
        outs = []
        for k in range(kept.shape[0]):
            order = [m for i in range(3) for m in lines[(i + k) % 3]]
            piece = double(halve(kept[k], order, place), list(reversed(order)), place)
            outs.append(double(piece, [1], place).astype(FLOAT))
        return outs

    output_grad, modulate_grad, query_grad = reduced(early)
    key_grad, value_grad = reduced(late)
    return (
        mixed,
        tokens_grad,
        query_grad,
        key_grad,
        value_grad,
        modulate_grad,
        output_grad,
        gate_grad,
        linear_grad,
        down_grad,
    )


def solution(mesh):
    return jax.shard_map(
        shards,
        mesh=mesh,
        in_specs=(
            P(("seq", "tp"), None),
            P(),
            P(),
            P(),
            P(),
            P(),
            P(None, "tp"),
            P(None, "tp"),
            P("tp", None),
            P(("seq", "tp"), None),
            P(),
        ),
        out_specs=(
            P(("seq", "tp"), None),
            P(("seq", "tp"), None),
            P(),
            P(),
            P(),
            P(),
            P(),
            P("seq", "tp"),
            P("seq", "tp"),
            P("tp", "seq"),
        ),
        check_vma=False,
    )
```

```python
import functools
import math

import jax
import jax.numpy as jnp
from jax import lax
from jax.experimental import pallas as pl
from jax.experimental.pallas import tpu as pltpu
from jax.sharding import PartitionSpec as P

BLOCK = 256
SEQ_LEN = 16384
EPS = 1e-06
FLOAT = jnp.float32
BHALF = jnp.bfloat16
VMEM_BYTES = 24 * 1024 * 1024


def bits_of(count):
    return [1 << b for b in range(count.bit_length() - 1)]


def swap(value, mask, axes=("seq", "tp")):
    count = lax.axis_size(axes)
    return lax.ppermute(value, axes, [(s, s ^ mask) for s in range(count)])


def bit_of(place, mask):
    return (place // mask) % 2


def after(value, *others):
    return lax.optimization_barrier((value,) + others)[0]


def halve(value, masks, place):
    for mask in masks:
        halves = value.reshape((2, value.shape[0] // 2) + value.shape[1:])
        bit = bit_of(place, mask)
        keep = lax.dynamic_index_in_dim(halves, bit, 0, False)
        send = lax.dynamic_index_in_dim(halves, 1 - bit, 0, False)
        value = (keep.astype(FLOAT) + swap(send, mask).astype(FLOAT)).astype(BHALF)
    return value


def double(value, masks, place):
    for mask in masks:
        other = swap(value, mask)
        bit = bit_of(place, mask)
        first = jnp.where(bit == 0, value, other)
        second = jnp.where(bit == 0, other, value)
        value = jnp.concatenate([first, second], axis=0)
    return value


def fold(value, masks):
    for mask in masks:
        half = value.shape[0] // 2
        got = swap(value[half:], mask)
        value = (value[:half].astype(FLOAT) + got.astype(FLOAT)).astype(BHALF)
    return value[0]


def decayed_scan(state, rate, unit, span, place, reverse):
    heads = state.shape[0]
    half = heads // 2
    bit = bit_of(place, 1)
    halves = state.reshape((2, half) + state.shape[1:])
    mine = lax.dynamic_index_in_dim(halves, bit, 0, False)
    theirs = lax.dynamic_index_in_dim(halves, 1 - bit, 0, False)
    other = swap(theirs.astype(BHALF), 1).astype(FLOAT)
    own_rate = lax.dynamic_index_in_dim(rate.reshape(2, half), bit, 0, False)

    def power(count):
        return jnp.exp2(-unit * count * own_rate)[:, None, None]

    later = 1 - bit if reverse else bit
    core_later = jnp.where(later == 1, mine, other)
    core_first = jnp.where(later == 1, other, mine)
    total = power(1.0) * core_first + core_later
    prefix = jnp.zeros_like(total)
    mark = None
    for mask in bits_of(span)[1:]:
        bit = bit_of(place, mask)
        later = 1 - bit if reverse else bit
        sent = swap(total.astype(BHALF), mask)
        mark = sent if mark is None else mark
        got = sent.astype(FLOAT)
        within = (place % mask) // 2
        if reverse:
            within = mask // 2 - 1 - within
        scale = power(2.0 * within.astype(FLOAT))
        prefix = prefix + jnp.where(later == 1, scale * got, 0.0)
        low = jnp.where(later == 1, got, total)
        high = jnp.where(later == 1, total, got)
        total = power(float(mask)) * low + high
    second_pre = power(1.0) * prefix + core_first
    bit = bit_of(place, 1)
    later = 1 - bit if reverse else bit
    own = jnp.where(later == 1, second_pre, prefix)
    away = jnp.where(later == 1, prefix, second_pre)
    got = swap(away.astype(BHALF), 1).astype(FLOAT)
    first = jnp.where(bit == 0, own, got)
    second = jnp.where(bit == 0, got, own)
    return jnp.concatenate([first, second], axis=0), mark


def gather_group(value, masks):
    rows = {0: value}
    for mask in masks:
        for r in list(rows):
            rows[r | mask] = swap(rows[r], mask)
    return [rows[r] for r in range(len(rows))]


def dot_nn(left, right):
    return jnp.dot(left, right, preferred_element_type=FLOAT)


def dot_tn(left, right):
    return lax.dot_general(left, right, (((0,), (0,)), ((), ())), preferred_element_type=FLOAT)


def dot_nt(left, right):
    return lax.dot_general(left, right, (((1,), (1,)), ((), ())), preferred_element_type=FLOAT)


def srms(values):
    return values * lax.rsqrt(jnp.mean(values * values, axis=-1, keepdims=True) + EPS)


def srms_back(values, gradient):
    scaled = lax.rsqrt(jnp.mean(values * values, axis=-1, keepdims=True) + EPS)
    normed = values * scaled
    return scaled * (gradient - normed * jnp.mean(gradient * normed, axis=-1, keepdims=True))


def swish(values):
    return values * jax.nn.sigmoid(values)


def swish_slope(values):
    sigmoid = jax.nn.sigmoid(values)
    return sigmoid * (1.0 + values * (1.0 - sigmoid))


def half_turn(values):
    return pltpu.roll(values, values.shape[-1] // 2, 1)


def rotate(values, cosine, sine):
    return values * cosine + half_turn(values) * sine


def unrotate(values, cosine, sine):
    return values * cosine - half_turn(values) * sine


def row_decay(rate, size, start, sign):
    offset = lax.broadcasted_iota(jnp.int32, (BLOCK, size), 0).astype(FLOAT)
    return jnp.exp2(-(start + sign * offset) * rate)


def query_decay(rate, size):
    return row_decay(rate, size, 1.0, 1.0)


def key_decay(rate, size):
    return row_decay(rate, size, BLOCK - 1.0, -1.0)


def decay_matrix(rate):
    row = lax.broadcasted_iota(jnp.int32, (BLOCK, BLOCK), 0)
    column = lax.broadcasted_iota(jnp.int32, (BLOCK, BLOCK), 1)
    distance = (row - column).astype(FLOAT)
    return jnp.where(distance >= 0.0, jnp.exp2(-jnp.maximum(distance, 0.0) * rate), 0.0)


def scaled_by(factor_exponent, values):
    return jnp.exp2(jnp.full(values.shape, factor_exponent, FLOAT)) * values


def shape_of(shape, dtype):
    return jax.ShapeDtypeStruct(shape, dtype)


SMEM_SPEC = pl.BlockSpec(memory_space=pltpu.SMEM)


def call(body, grid, in_specs, out_specs, out_shape, flops, moved, scratch=(), vmem=VMEM_BYTES):
    return pl.pallas_call(
        body,
        grid=grid,
        in_specs=in_specs,
        out_specs=out_specs,
        out_shape=out_shape,
        scratch_shapes=scratch,
        cost_estimate=pl.CostEstimate(flops=flops, bytes_accessed=moved, transcendentals=0),
        compiler_params=pltpu.CompilerParams(vmem_limit_bytes=vmem),
    )


def kv_body(heads, rate, x, wk, wv, cosine, sine, normed, pre_key, keys, values, contrib, local):
    step = pl.program_id(0)
    size = cosine.shape[1]
    blocks = x.shape[0] // BLOCK

    @pl.when(step == 0)
    def _():
        normed[...] = srms(x[...].astype(FLOAT)).astype(BHALF)

    rows = normed[...]
    pre = dot_nn(rows, wk[...])
    pre_key[...] = pre
    val = dot_nn(rows, wv[...]).astype(BHALF)
    values[...] = val
    for h in range(heads):
        part = slice(h * size, (h + 1) * size)
        own_rate = rate[step * heads + h]
        key = rotate(swish(pre[:, part]), cosine[...], sine[...]).astype(BHALF)
        keys[:, part] = key
        decay = key_decay(own_rate, size)
        total = None
        for b in range(blocks):
            span = slice(b * BLOCK, (b + 1) * BLOCK)
            decayed = (key[span].astype(FLOAT) * decay).astype(BHALF)
            state = dot_tn(decayed, val[span, part])
            contrib[b, h] = state
            total = state if total is None else scaled_by(-BLOCK * own_rate, total) + state
        local[h] = total


def kv(rate, x, wk, wv, cosine, sine, steps):
    tokens, width = x.shape
    heads = rate.shape[0]
    size = width // heads
    group = heads // steps
    cols = group * size
    blocks = tokens // BLOCK
    tile = lambda n: pl.BlockSpec((n, cols), lambda i: (0, i))
    whole = lambda a: pl.BlockSpec(a.shape, lambda i: (0, 0))
    return call(
        functools.partial(kv_body, group),
        (steps,),
        [SMEM_SPEC, whole(x), tile(width), tile(width), whole(cosine), whole(sine)],
        [
            whole(x),
            tile(tokens),
            tile(tokens),
            tile(tokens),
            pl.BlockSpec((blocks, group, size, size), lambda i: (0, i, 0, 0)),
            pl.BlockSpec((group, size, size), lambda i: (i, 0, 0)),
        ],
        [
            shape_of(x.shape, BHALF),
            shape_of(x.shape, FLOAT),
            shape_of(x.shape, BHALF),
            shape_of(x.shape, BHALF),
            shape_of((blocks, heads, size, size), FLOAT),
            shape_of((heads, size, size), FLOAT),
        ],
        4 * tokens * width * width,
        12 * tokens * width + 4 * width * width,
    )(rate, x, wk, wv, cosine, sine)


def qu_body(heads, rate, rows, wq, wu, cosine, sine, keys, values, pre_query, query, gate, intra):
    step = pl.program_id(0)
    size = cosine.shape[1]
    blocks = rows.shape[0] // BLOCK
    pre = dot_nn(rows[...], wq[...])
    pre_query[...] = pre
    gate[...] = dot_nn(rows[...], wu[...])
    for h in range(heads):
        part = slice(h * size, (h + 1) * size)
        q = rotate(swish(pre[:, part]), cosine[...], sine[...]).astype(BHALF)
        query[:, part] = q
        decay = decay_matrix(rate[step * heads + h])
        for b in range(blocks):
            span = slice(b * BLOCK, (b + 1) * BLOCK)
            weights = (dot_nt(q[span], keys[span, part]) * decay).astype(BHALF)
            intra[span, part] = dot_nn(weights, values[span, part])


def qu(rate, rows, wq, wu, cosine, sine, keys, values, steps):
    tokens, width = rows.shape
    heads = rate.shape[0]
    group = heads // steps
    cols = group * (width // heads)
    tile = lambda n: pl.BlockSpec((n, cols), lambda i: (0, i))
    whole = lambda a: pl.BlockSpec(a.shape, lambda i: (0, 0))
    return call(
        functools.partial(qu_body, group),
        (steps,),
        [SMEM_SPEC, whole(rows), tile(width), tile(width), whole(cosine), whole(sine)]
        + [tile(tokens)] * 2,
        [tile(tokens)] * 4,
        [shape_of(rows.shape, d) for d in (FLOAT, BHALF, FLOAT, FLOAT)],
        4 * tokens * width * width,
        20 * tokens * width + 4 * width * width,
    )(rate, rows, wq, wu, cosine, sine, keys, values)


def join_body(heads, use_next, rate, x, intra, query, gate, state, before, wo, *outs):
    attended, gated, resid, normed, used = outs
    size = state.shape[1]
    pieces = []
    for h in range(heads):
        part = slice(h * size, (h + 1) * size)
        own_rate = rate[h]
        here = state[h]
        if use_next:
            here = scaled_by(-BLOCK * own_rate, here) + before[h]
        here = here.astype(BHALF)
        used[h] = here
        q = (query[:, part].astype(FLOAT) * query_decay(own_rate, size)).astype(BHALF)
        pieces.append(intra[:, part] + dot_nn(q, here))
    full = jnp.concatenate(pieces, axis=1)
    attended[...] = full
    g = (srms(full) * gate[...]).astype(BHALF)
    gated[...] = g
    r = x[...].astype(FLOAT) + dot_nn(g, wo[...])
    resid[...] = r
    normed[...] = srms(r).astype(BHALF)


def join(block, rate, x, intra, query, gate, state, contrib, wo):
    width = x.shape[1]
    heads, size = state.shape[0], state.shape[1]
    before = contrib
    if block > 1:
        for b in range(block - 1):
            state = jnp.exp2(-BLOCK * rate)[:, None, None] * state + contrib[b]
    row = pl.BlockSpec((BLOCK, width), lambda i: (block, 0))
    out_row = pl.BlockSpec((BLOCK, width), lambda i: (0, 0))
    cube = pl.BlockSpec((heads, size, size), lambda i: (0, 0, 0))
    earlier = max(block - 1, 0)
    return call(
        functools.partial(join_body, heads, block > 0),
        (1,),
        [SMEM_SPEC, row, row, row, row, cube]
        + [pl.BlockSpec((None, heads, size, size), lambda i: (earlier, 0, 0, 0))]
        + [pl.BlockSpec(wo.shape, lambda i: (0, 0))],
        [out_row] * 4 + [cube],
        [shape_of((BLOCK, width), d) for d in (FLOAT, BHALF, FLOAT, BHALF)]
        + [shape_of((heads, size, size), BHALF)],
        2 * BLOCK * width * (width + size),
        24 * BLOCK * width + 2 * width * width,
    )(rate, x, intra, query, gate, state, before, wo)


def unit_body(n0, n1, c0, c1, gate_t, linear_t, down, keep, ship, hidden, gate_back, linear_back):
    rows = jnp.concatenate([n0[...], n1[...]], axis=0)
    cots = jnp.concatenate([c0[...], c1[...]], axis=0)
    gate = dot_nt(rows, gate_t[...])
    linear = dot_nt(rows, linear_t[...])
    inner = (gate * linear).astype(BHALF)
    hidden[...] = inner
    inner_cot = dot_nt(cots, down[...])
    gb = (inner_cot * linear).astype(BHALF)
    lb = (inner_cot * gate).astype(BHALF)
    gate_back[...] = gb
    linear_back[...] = lb
    feed = dot_nn(inner, down[...])
    cot = dot_nn(gb, gate_t[...]) + dot_nn(lb, linear_t[...])
    keep[0] = cot[:BLOCK]
    keep[1] = feed[:BLOCK]
    ship[0] = cot[BLOCK:].astype(BHALF)
    ship[1] = feed[BLOCK:].astype(BHALF)


def unit(block, rows, cots, gate_t, linear_t, down):
    width = rows[0].shape[1]
    inner = down.shape[0]
    piece = pl.BlockSpec((BLOCK, width), lambda i: (0, 0))
    cot = pl.BlockSpec((BLOCK, width), lambda i: (block, 0))
    whole = lambda s: pl.BlockSpec(s, lambda i: (0,) * len(s))
    wide = (2 * BLOCK, inner)
    pair = (2, BLOCK, width)
    return call(
        unit_body,
        (1,),
        [piece] * 2 + [cot] * 2 + [whole(down.shape)] * 3,
        [whole(pair)] * 2 + [whole(wide)] * 3,
        [shape_of(pair, FLOAT), shape_of(pair, BHALF)] + [shape_of(wide, BHALF)] * 3,
        24 * BLOCK * width * inner,
        6 * width * inner + 20 * BLOCK * width,
    )(*rows, *cots, gate_t, linear_t, down)


def place_in(order, count, shard, place):
    relative = jnp.bitwise_xor(shard, place)
    position = 0
    for mask in order:
        position = position * 2 + jnp.bitwise_and(relative // mask, 1)
    return position


def unit_grads_body(groups, orders, place, *refs):
    per = 2 + 2 + 3
    ins = refs[: groups * per]
    pair_out, down_out = refs[groups * per : groups * per + 2]
    rows, cots, hidden, gate_back, linear_back, sems = refs[groups * per + 2 :]
    copies = [[] for _ in range(groups)]
    for g in range(groups):
        n0, n1, c0, c1, h, gb, lb = ins[g * per : (g + 1) * per]
        block = g % 2
        span = pl.ds(block * BLOCK, BLOCK)
        moves = [
            (gb, gate_back.at[g]),
            (n0, rows.at[g, pl.ds(0, BLOCK)]),
            (n1, rows.at[g, pl.ds(BLOCK, BLOCK)]),
            (lb, linear_back.at[g]),
            (h, hidden.at[g]),
            (c0.at[span], cots.at[g, pl.ds(0, BLOCK)]),
            (c1.at[span], cots.at[g, pl.ds(BLOCK, BLOCK)]),
        ]
        for k, (source, target) in enumerate(moves):
            copies[g].append(pltpu.make_async_copy(source, target, sems.at[g, k]))
    for first, last in ((0, 3), (3, 4), (4, 7)):
        for g in range(groups):
            for copy in copies[g][first:last]:
                copy.start()
    count = pair_out.shape[0]
    here = place[0]

    def total(left, right, first, last):
        acc = None
        for g in range(groups):
            for copy in copies[g][first:last]:
                copy.wait()
            term = dot_tn(left[g], right[g])
            acc = term if acc is None else acc + term
        return acc

    def store(acc, put, order):
        size = acc.shape[1] // count
        for shard in range(count):
            put(place_in(order, count, shard, here), acc[:, shard * size : (shard + 1) * size])

    def put_pair(k):
        def put(position, value):
            pair_out[position, k] = value.astype(BHALF)
        return put

    def put_down(position, value):
        down_out[position] = value.astype(BHALF)

    store(total(gate_back, rows, 0, 3), put_pair(0), orders[0])
    store(total(linear_back, rows, 3, 4), put_pair(1), orders[0])
    store(total(hidden, cots, 4, 7), put_down, orders[1])


def unit_grads(place, groups, orders, count):
    inner = groups[0][4].shape[1]
    width = groups[0][0].shape[1]
    flat = [a for group in groups for a in group]
    any_spec = pl.BlockSpec(memory_space=pl.ANY)
    size = width // count
    pair = (count, 2, inner, size)
    single = (count, inner, size)
    n = len(groups)
    whole = lambda s: pl.BlockSpec(s, lambda i: (0,) * len(s))
    return call(
        functools.partial(unit_grads_body, n, orders),
        (1,),
        [SMEM_SPEC] + [any_spec] * len(flat),
        [whole(pair), whole(single)],
        [shape_of(pair, BHALF), shape_of(single, BHALF)],
        12 * n * BLOCK * width * inner,
        n * 2 * BLOCK * (4 * width + 6 * inner) + 6 * width * inner,
        scratch=[
            pltpu.VMEM((n, 2 * BLOCK, width), BHALF),
            pltpu.VMEM((n, 2 * BLOCK, width), BHALF),
            pltpu.VMEM((n, 2 * BLOCK, inner), BHALF),
            pltpu.VMEM((n, 2 * BLOCK, inner), BHALF),
            pltpu.VMEM((n, 2 * BLOCK, inner), BHALF),
            pltpu.SemaphoreType.DMA((n, 7)),
        ],
        vmem=VMEM_BYTES if n <= 4 else 2 * VMEM_BYTES,
    )(place, *flat)


def turn_body(heads, rate, keep, got, far, resid, cot, attended, gate, query, wo, *outs):
    resid_cot, branch, modulate, back, direct = outs
    size = direct.shape[1]
    normed_cot = keep[0] + got[0].astype(FLOAT)
    for k in range(far.shape[0]):
        normed_cot = normed_cot + far[k].astype(FLOAT)
    rc = cot[...].astype(FLOAT) + srms_back(resid[...], normed_cot)
    resid_cot[...] = rc
    bb = rc.astype(BHALF)
    branch[...] = bb
    gated_cot = dot_nt(bb, wo[...])
    att = attended[...]
    modulate[...] = (gated_cot * srms(att)).astype(BHALF)
    ab = srms_back(att, gated_cot * gate[...]).astype(BHALF)
    back[...] = ab
    for h in range(heads):
        part = slice(h * size, (h + 1) * size)
        q = (query[:, part].astype(FLOAT) * query_decay(rate[h], size)).astype(BHALF)
        direct[h] = dot_tn(q, ab[:, part])


def turn(block, rate, keep, got, far, resid, cot, attended, gate, query, wo):
    width = resid.shape[1]
    heads = rate.shape[0]
    size = width // heads
    row = pl.BlockSpec((BLOCK, width), lambda i: (block, 0))
    own = pl.BlockSpec((BLOCK, width), lambda i: (0, 0))
    first = pl.BlockSpec((1, BLOCK, width), lambda i: (0, 0, 0))
    cube = pl.BlockSpec((heads, size, size), lambda i: (0, 0, 0))
    return call(
        functools.partial(turn_body, heads),
        (1,),
        [SMEM_SPEC, first, first, pl.BlockSpec(far.shape, lambda i: (0, 0, 0)), own, row, own]
        + [row, row, pl.BlockSpec(wo.shape, lambda i: (0, 0))],
        [own] * 4 + [cube],
        [shape_of((BLOCK, width), d) for d in (FLOAT, BHALF, BHALF, BHALF)]
        + [shape_of((heads, size, size), FLOAT)],
        2 * BLOCK * width * (width + size),
        32 * BLOCK * width + 2 * width * width,
    )(rate, keep, got, far, resid, cot, attended, gate, query, wo)


def query_body(heads, blocks, rate, pre_query, query, keys, values, cosine, sine, *refs):
    backs = refs[:blocks]
    used = refs[blocks : 2 * blocks]
    query_back, key_part, value_part = refs[2 * blocks :]
    step = pl.program_id(0)
    size = cosine.shape[1]
    for h in range(heads):
        part = slice(h * size, (h + 1) * size)
        own_rate = rate[step * heads + h]
        decay = decay_matrix(own_rate)
        row = query_decay(own_rate, size)
        for b in range(blocks):
            span = slice(b * BLOCK, (b + 1) * BLOCK)
            q, k, v = query[span, part], keys[span, part], values[span, part]
            ab = backs[b][:, part]
            weights = (dot_nt(q, k) * decay).astype(BHALF)
            weights_back = (dot_nt(ab, v) * decay).astype(BHALF)
            value_part[span, part] = dot_tn(weights, ab)
            key_part[span, part] = dot_tn(weights_back, q)
            cot = dot_nn(weights_back, k) + row * dot_nt(ab, used[b][h])
            cot = unrotate(cot, cosine[span], sine[span])
            query_back[span, part] = (cot * swish_slope(pre_query[span, part])).astype(BHALF)


def query_side(rate, pre_query, query, keys, values, cosine, sine, backs, used, steps):
    tokens, width = query.shape
    heads = rate.shape[0]
    size = width // heads
    group = heads // steps
    cols = group * size
    blocks = len(backs)
    tile = pl.BlockSpec((tokens, cols), lambda i: (0, i))
    whole = lambda a: pl.BlockSpec(a.shape, lambda i: (0, 0))
    return call(
        functools.partial(query_body, group, blocks),
        (steps,),
        [SMEM_SPEC] + [tile] * 4 + [whole(cosine), whole(sine)]
        + [pl.BlockSpec((BLOCK, cols), lambda i: (0, i))] * blocks
        + [pl.BlockSpec((group, size, size), lambda i: (i, 0, 0))] * blocks,
        [tile] * 3,
        [shape_of(query.shape, d) for d in (BHALF, FLOAT, FLOAT)],
        12 * tokens * width * BLOCK,
        24 * tokens * width,
    )(rate, pre_query, query, keys, values, cosine, sine, *backs, *used)


def key_body(heads, blocks, rate, pre_key, keys, values, key_part, value_part, *refs):
    cosine, sine, state = refs[:3]
    direct = refs[3 : 3 + blocks]
    key_back, value_back = refs[3 + blocks :]
    step = pl.program_id(0)
    size = cosine.shape[1]
    for h in range(heads):
        part = slice(h * size, (h + 1) * size)
        own_rate = rate[step * heads + h]
        decay = key_decay(own_rate, size)
        here = state[h]
        for b in reversed(range(blocks)):
            span = slice(b * BLOCK, (b + 1) * BLOCK)
            used = here.astype(BHALF)
            cot = key_part[span, part] + decay * dot_nt(values[span, part], used)
            decayed = (keys[span, part].astype(FLOAT) * decay).astype(BHALF)
            vcot = value_part[span, part] + dot_nn(decayed, used)
            cot = unrotate(cot, cosine[span], sine[span])
            key_back[span, part] = (cot * swish_slope(pre_key[span, part])).astype(BHALF)
            value_back[span, part] = vcot.astype(BHALF)
            if b:
                here = scaled_by(-BLOCK * own_rate, here) + direct[b][h]


def key_side(rate, pre_key, keys, values, key_part, value_part, cosine, sine, state, direct, steps):
    tokens, width = keys.shape
    heads = rate.shape[0]
    size = width // heads
    group = heads // steps
    cols = group * size
    blocks = len(direct)
    tile = pl.BlockSpec((tokens, cols), lambda i: (0, i))
    whole = lambda a: pl.BlockSpec(a.shape, lambda i: (0, 0))
    cube = pl.BlockSpec((group, size, size), lambda i: (i, 0, 0))
    return call(
        functools.partial(key_body, group, blocks),
        (steps,),
        [SMEM_SPEC] + [tile] * 5 + [whole(cosine), whole(sine), cube] + [cube] * blocks,
        [tile] * 2,
        [shape_of(keys.shape, BHALF)] * 2,
        4 * tokens * width * size,
        20 * tokens * width,
    )(rate, pre_key, keys, values, key_part, value_part, cosine, sine, state, *direct)


def grads_body(lefts, pairs, core, *refs):
    left = refs[:lefts]
    right = refs[lefts:-1]
    out = refs[-1]
    for k, (l, rs) in enumerate(pairs):
        acc = None
        start = 0
        for piece in rs:
            r = right[piece]
            rows = r.shape[0]
            term = dot_tn(left[l][start : start + rows], r[...])
            start += rows
            acc = term if acc is None else acc + term
        out[0, k] = acc.astype(BHALF)


def grads(core, lefts, rights, pairs):
    tokens, width = lefts[0].shape
    cols = rights[0].shape[1]
    half = width // 2
    spec = pltpu.PrefetchScalarGridSpec(
        num_scalar_prefetch=1,
        grid=(2,),
        in_specs=[pl.BlockSpec((tokens, half), lambda i, c: (0, i ^ c[0]))] * len(lefts)
        + [pl.BlockSpec(r.shape, lambda i, c: (0, 0)) for r in rights],
        out_specs=pl.BlockSpec((1, len(pairs), half, cols), lambda i, c: (i, 0, 0, 0)),
    )
    n = len(pairs)
    body = functools.partial(grads_body, len(lefts), pairs)
    return pl.pallas_call(
        body,
        grid_spec=spec,
        out_shape=shape_of((2, n, half, cols), BHALF),
        cost_estimate=pl.CostEstimate(
            flops=2 * n * tokens * width * cols, bytes_accessed=4 * n * width * cols, transcendentals=0
        ),
        compiler_params=pltpu.CompilerParams(vmem_limit_bytes=VMEM_BYTES),
    )(core, *lefts, *rights)


def tokens_body(x, rc, qb, kb, vb, mb, wq, wk, wv, wm, out):
    grad = dot_nt(qb[...], wq[...]) + dot_nt(kb[...], wk[...])
    grad = grad + dot_nt(vb[...], wv[...]) + dot_nt(mb[...], wm[...])
    out[...] = rc[...] + srms_back(x[...].astype(FLOAT), grad)


def tokens_side(block, x, rc, qb, kb, vb, mb, weights):
    tokens, width = x.shape
    row = pl.BlockSpec((BLOCK, width), lambda i: (block, 0))
    own = pl.BlockSpec((BLOCK, width), lambda i: (0, 0))
    whole = pl.BlockSpec((width, width), lambda i: (0, 0))
    return call(
        tokens_body,
        (1,),
        [row, own, row, row, row, own] + [whole] * 4,
        own,
        shape_of((BLOCK, width), FLOAT),
        8 * BLOCK * width * width,
        8 * width * width + 20 * BLOCK * width,
    )(x, rc, qb, kb, vb, mb, *weights)


def angle_tables(position, halves):
    column = jnp.arange(halves, dtype=jnp.int32)
    factor = 1 + jnp.right_shift(jnp.full((halves,), 16384, jnp.int32), column // 4)
    phase = position[:, None] * factor[None, :] % 65536
    turned = phase.astype(FLOAT) * (2.0 * math.pi / 65536.0)
    cosine, sine = jnp.cos(turned), jnp.sin(turned)
    return jnp.concatenate([cosine, cosine], 1), jnp.concatenate([-sine, sine], 1)


def shards(
    tokens,
    query_weight,
    key_weight,
    value_weight,
    modulate_weight,
    output_weight,
    gate_weight,
    linear_weight,
    down_weight,
    cotangent,
    decay_exponent,
):
    count, width = tokens.shape
    heads = decay_exponent.shape[0]
    size = width // heads
    runs, members = lax.axis_size("seq"), lax.axis_size("tp")
    devices = runs * members
    length = min(SEQ_LEN, count * devices)
    span = length // count
    blocks = count // BLOCK
    seq_place = lax.axis_index("seq")
    place = seq_place * members + lax.axis_index("tp")
    core = bit_of(place, 1).astype(jnp.int32).reshape(1)
    position = (place * count + jnp.arange(count, dtype=jnp.int32)) % length
    rate = jnp.exp2(-decay_exponent.astype(FLOAT))
    cosine, sine = angle_tables(position, size // 2)
    ring = bits_of(members)
    far = ring[1:]

    normed, pre_key, keys, values, contrib, local = kv(
        rate, tokens, key_weight, value_weight, cosine, sine, 2
    )
    state, mark = decayed_scan(local, rate, float(count), span, place, False)
    pre_query, query, gate, intra = qu(
        rate, normed, query_weight, modulate_weight, cosine, sine, keys, values, 2
    )
    cots = gather_group(after(cotangent, mark), far + [1])
    joined = [
        join(b, rate, tokens, intra, query, gate, state, contrib, output_weight)
        for b in range(blocks)
    ]

    gate_t, linear_t = gate_weight.T, linear_weight.T
    gathered = [gather_group(joined[b][3], far + [1]) for b in range(blocks)]
    results = {}
    for r in range(0, members, 2):
        for b in range(blocks):
            results[r, b] = unit(
                b, gathered[b][r : r + 2], cots[r : r + 2], gate_t, linear_t, down_weight
            )
    groups = [
        tuple(gathered[b][r : r + 2]) + tuple(cots[r : r + 2]) + tuple(results[r, b][2:])
        for r in range(0, members, 2)
        for b in range(blocks)
    ]
    near = {}
    for key, value in results.items():
        near[key] = (value[0], swap(value[1], 1))
    arrived = {}
    for part in range(2):
        for b in range(blocks):
            rows = {
                r: near[r, b][0][part] + near[r, b][1][part].astype(FLOAT)
                for r in range(2, members, 2)
            }
            got = []
            for mask in reversed(far):
                for r in [r for r in rows if r & mask]:
                    value = swap(rows.pop(r).astype(BHALF), mask)
                    if r == mask:
                        got.append(value)
                    else:
                        rows[r ^ mask] = rows[r ^ mask] + value.astype(FLOAT)
            arrived[b, part] = got

    turned = [
        turn(
            b, rate, near[0, b][0], near[0, b][1], jnp.stack(arrived[b, 0]), joined[b][2],
            cotangent, joined[b][0], gate, query, output_weight,
        )
        for b in range(blocks)
    ]
    line = bits_of(runs)
    across = max(members // 2, 1)
    orders = (line, [m for m in line if m >= across] + [m for m in line if m < across])
    seq_scalar = seq_place.astype(jnp.int32).reshape(1)
    pair_part, down_part = unit_grads(seq_scalar, groups, orders, runs)

    decays = jnp.exp2(-BLOCK * rate)[:, None, None]
    inbound = turned[blocks - 1][4]
    for b in reversed(range(blocks - 1)):
        inbound = decays * inbound + turned[b][4]
    outer, _ = decayed_scan(inbound, rate, float(count), span, place, True)
    backs = [t[3] for t in turned]
    query_back, key_part, value_part = query_side(
        rate, pre_query, query, keys, values, cosine, sine, backs, [j[4] for j in joined], 2
    )
    gated = jnp.concatenate([j[1] for j in joined], axis=0)
    early = grads(
        core,
        [gated, normed],
        [t[1] for t in turned] + [t[2] for t in turned] + [query_back],
        [
            (0, list(range(blocks))),
            (1, list(range(blocks, 2 * blocks))),
            (1, [2 * blocks]),
        ],
    )
    key_back, value_back = key_side(
        rate, pre_key, keys, values, key_part, value_part, cosine, sine, outer,
        [t[4] for t in turned], 2,
    )
    late = grads(core, [normed], [key_back, value_back], [(0, [0]), (0, [1])])
    weights = (query_weight, key_weight, value_weight, modulate_weight)
    tokens_grad = jnp.concatenate(
        [
            tokens_side(
                b, tokens, turned[b][0], query_back, key_back, value_back, turned[b][2], weights
            )
            for b in range(blocks)
        ],
        axis=0,
    )

    mixed = jnp.concatenate(
        [
            (
                joined[b][2] + near[0, b][0][1] + near[0, b][1][1].astype(FLOAT)
                + sum(a.astype(FLOAT) for a in arrived[b, 1])
            ).astype(BHALF)
            for b in range(blocks)
        ],
        axis=0,
    )
    masks = [[members * m for m in order] for order in orders]
    pair_grad = fold(pair_part, masks[0]).astype(FLOAT)
    down_grad = fold(down_part, masks[1]).astype(FLOAT)
    gate_grad, linear_grad = pair_grad[0].T, pair_grad[1].T

    rest = bits_of(devices)[1:]
    lines = [
        [m for m in rest if m < members],
        [m for m in rest if members <= m < members * across],
        [m for m in rest if m >= members * across],
    ]

    def reduced(part):
        kept = (part[0].astype(FLOAT) + swap(part[1], 1).astype(FLOAT)).astype(BHALF)
        outs = []
        for k in range(kept.shape[0]):
            order = [m for i in range(3) for m in lines[(i + k) % 3]]
            piece = double(halve(kept[k], order, place), list(reversed(order)), place)
            outs.append(double(piece, [1], place).astype(FLOAT))
        return outs

    output_grad, modulate_grad, query_grad = reduced(early)
    key_grad, value_grad = reduced(late)
    return (
        mixed,
        tokens_grad,
        query_grad,
        key_grad,
        value_grad,
        modulate_grad,
        output_grad,
        gate_grad,
        linear_grad,
        down_grad,
    )


def solution(mesh):
    return jax.shard_map(
        shards,
        mesh=mesh,
        in_specs=(
            P(("seq", "tp"), None),
            P(),
            P(),
            P(),
            P(),
            P(),
            P(None, "tp"),
            P(None, "tp"),
            P("tp", None),
            P(("seq", "tp"), None),
            P(),
        ),
        out_specs=(
            P(("seq", "tp"), None),
            P(("seq", "tp"), None),
            P(),
            P(),
            P(),
            P(),
            P(),
            P("seq", "tp"),
            P("seq", "tp"),
            P("tp", "seq"),
        ),
        check_vma=False,
    )
```

```python
import functools
import math

import jax
import jax.numpy as jnp
from jax import lax
from jax.experimental import pallas as pl
from jax.experimental.pallas import tpu as pltpu
from jax.sharding import PartitionSpec as P

BLOCK = 256
SEQ_LEN = 16384
EPS = 1e-06
FLOAT = jnp.float32
BHALF = jnp.bfloat16
VMEM_BYTES = 24 * 1024 * 1024


def bits_of(count):
    return [1 << b for b in range(count.bit_length() - 1)]


def swap(value, mask, axes=("seq", "tp")):
    count = lax.axis_size(axes)
    return lax.ppermute(value, axes, [(s, s ^ mask) for s in range(count)])


def bit_of(place, mask):
    return (place // mask) % 2


def after(value, *others):
    return lax.optimization_barrier((value,) + others)[0]


def halve(value, masks, place):
    for mask in masks:
        halves = value.reshape((2, value.shape[0] // 2) + value.shape[1:])
        bit = bit_of(place, mask)
        keep = lax.dynamic_index_in_dim(halves, bit, 0, False)
        send = lax.dynamic_index_in_dim(halves, 1 - bit, 0, False)
        value = (keep.astype(FLOAT) + swap(send, mask).astype(FLOAT)).astype(BHALF)
    return value


def double(value, masks, place):
    for mask in masks:
        other = swap(value, mask)
        bit = bit_of(place, mask)
        first = jnp.where(bit == 0, value, other)
        second = jnp.where(bit == 0, other, value)
        value = jnp.concatenate([first, second], axis=0)
    return value


def fold(value, masks):
    for mask in masks:
        half = value.shape[0] // 2
        got = swap(value[half:], mask)
        value = (value[:half].astype(FLOAT) + got.astype(FLOAT)).astype(BHALF)
    return value[0]


def decayed_scan(state, rate, unit, span, place, reverse):
    heads = state.shape[0]
    half = heads // 2
    bit = bit_of(place, 1)
    halves = state.reshape((2, half) + state.shape[1:])
    mine = lax.dynamic_index_in_dim(halves, bit, 0, False)
    theirs = lax.dynamic_index_in_dim(halves, 1 - bit, 0, False)
    other = swap(theirs.astype(BHALF), 1).astype(FLOAT)
    own_rate = lax.dynamic_index_in_dim(rate.reshape(2, half), bit, 0, False)

    def power(count):
        return jnp.exp2(-unit * count * own_rate)[:, None, None]

    later = 1 - bit if reverse else bit
    core_later = jnp.where(later == 1, mine, other)
    core_first = jnp.where(later == 1, other, mine)
    total = power(1.0) * core_first + core_later
    prefix = jnp.zeros_like(total)
    mark = None
    for mask in bits_of(span)[1:]:
        bit = bit_of(place, mask)
        later = 1 - bit if reverse else bit
        sent = swap(total.astype(BHALF), mask)
        mark = sent if mark is None else mark
        got = sent.astype(FLOAT)
        within = (place % mask) // 2
        if reverse:
            within = mask // 2 - 1 - within
        scale = power(2.0 * within.astype(FLOAT))
        prefix = prefix + jnp.where(later == 1, scale * got, 0.0)
        low = jnp.where(later == 1, got, total)
        high = jnp.where(later == 1, total, got)
        total = power(float(mask)) * low + high
    second_pre = power(1.0) * prefix + core_first
    bit = bit_of(place, 1)
    later = 1 - bit if reverse else bit
    own = jnp.where(later == 1, second_pre, prefix)
    away = jnp.where(later == 1, prefix, second_pre)
    got = swap(away.astype(BHALF), 1).astype(FLOAT)
    first = jnp.where(bit == 0, own, got)
    second = jnp.where(bit == 0, got, own)
    return jnp.concatenate([first, second], axis=0), mark


def gather_group(value, masks):
    rows = {0: value}
    for mask in masks:
        for r in list(rows):
            rows[r | mask] = swap(rows[r], mask)
    return [rows[r] for r in range(len(rows))]


def dot_nn(left, right):
    return jnp.dot(left, right, preferred_element_type=FLOAT)


def dot_tn(left, right):
    return lax.dot_general(left, right, (((0,), (0,)), ((), ())), preferred_element_type=FLOAT)


def dot_nt(left, right):
    return lax.dot_general(left, right, (((1,), (1,)), ((), ())), preferred_element_type=FLOAT)


def srms(values):
    return values * lax.rsqrt(jnp.mean(values * values, axis=-1, keepdims=True) + EPS)


def srms_back(values, gradient):
    scaled = lax.rsqrt(jnp.mean(values * values, axis=-1, keepdims=True) + EPS)
    normed = values * scaled
    return scaled * (gradient - normed * jnp.mean(gradient * normed, axis=-1, keepdims=True))


def swish(values):
    return values * jax.nn.sigmoid(values)


def swish_slope(values):
    sigmoid = jax.nn.sigmoid(values)
    return sigmoid * (1.0 + values * (1.0 - sigmoid))


def half_turn(values):
    return pltpu.roll(values, values.shape[-1] // 2, 1)


def rotate(values, cosine, sine):
    return values * cosine + half_turn(values) * sine


def unrotate(values, cosine, sine):
    return values * cosine - half_turn(values) * sine


def row_decay(rate, size, start, sign):
    offset = lax.broadcasted_iota(jnp.int32, (BLOCK, size), 0).astype(FLOAT)
    return jnp.exp2(-(start + sign * offset) * rate)


def query_decay(rate, size):
    return row_decay(rate, size, 1.0, 1.0)


def key_decay(rate, size):
    return row_decay(rate, size, BLOCK - 1.0, -1.0)


def decay_matrix(rate):
    row = lax.broadcasted_iota(jnp.int32, (BLOCK, BLOCK), 0)
    column = lax.broadcasted_iota(jnp.int32, (BLOCK, BLOCK), 1)
    distance = (row - column).astype(FLOAT)
    return jnp.where(distance >= 0.0, jnp.exp2(-jnp.maximum(distance, 0.0) * rate), 0.0)


def scaled_by(factor_exponent, values):
    return jnp.exp2(jnp.full(values.shape, factor_exponent, FLOAT)) * values


def shape_of(shape, dtype):
    return jax.ShapeDtypeStruct(shape, dtype)


SMEM_SPEC = pl.BlockSpec(memory_space=pltpu.SMEM)


def call(body, grid, in_specs, out_specs, out_shape, flops, moved, scratch=(), vmem=VMEM_BYTES):
    return pl.pallas_call(
        body,
        grid=grid,
        in_specs=in_specs,
        out_specs=out_specs,
        out_shape=out_shape,
        scratch_shapes=scratch,
        cost_estimate=pl.CostEstimate(flops=flops, bytes_accessed=moved, transcendentals=0),
        compiler_params=pltpu.CompilerParams(vmem_limit_bytes=vmem),
    )


def kv_body(heads, rate, x, wk, wv, cosine, sine, normed, pre_key, keys, values, contrib, local):
    step = pl.program_id(0)
    size = cosine.shape[1]
    blocks = x.shape[0] // BLOCK

    @pl.when(step == 0)
    def _():
        normed[...] = srms(x[...].astype(FLOAT)).astype(BHALF)

    rows = normed[...]
    pre = dot_nn(rows, wk[...])
    pre_key[...] = pre
    val = dot_nn(rows, wv[...]).astype(BHALF)
    values[...] = val
    for h in range(heads):
        part = slice(h * size, (h + 1) * size)
        own_rate = rate[step * heads + h]
        key = rotate(swish(pre[:, part]), cosine[...], sine[...]).astype(BHALF)
        keys[:, part] = key
        decay = key_decay(own_rate, size)
        total = None
        for b in range(blocks):
            span = slice(b * BLOCK, (b + 1) * BLOCK)
            decayed = (key[span].astype(FLOAT) * decay).astype(BHALF)
            state = dot_tn(decayed, val[span, part])
            contrib[b, h] = state
            total = state if total is None else scaled_by(-BLOCK * own_rate, total) + state
        local[h] = total


def kv(rate, x, wk, wv, cosine, sine, steps):
    tokens, width = x.shape
    heads = rate.shape[0]
    size = width // heads
    group = heads // steps
    cols = group * size
    blocks = tokens // BLOCK
    tile = lambda n: pl.BlockSpec((n, cols), lambda i: (0, i))
    whole = lambda a: pl.BlockSpec(a.shape, lambda i: (0, 0))
    return call(
        functools.partial(kv_body, group),
        (steps,),
        [SMEM_SPEC, whole(x), tile(width), tile(width), whole(cosine), whole(sine)],
        [
            whole(x),
            tile(tokens),
            tile(tokens),
            tile(tokens),
            pl.BlockSpec((blocks, group, size, size), lambda i: (0, i, 0, 0)),
            pl.BlockSpec((group, size, size), lambda i: (i, 0, 0)),
        ],
        [
            shape_of(x.shape, BHALF),
            shape_of(x.shape, FLOAT),
            shape_of(x.shape, BHALF),
            shape_of(x.shape, BHALF),
            shape_of((blocks, heads, size, size), FLOAT),
            shape_of((heads, size, size), FLOAT),
        ],
        4 * tokens * width * width,
        12 * tokens * width + 4 * width * width,
    )(rate, x, wk, wv, cosine, sine)


def qu_body(heads, rate, rows, wq, wu, cosine, sine, keys, values, pre_query, query, gate, intra):
    step = pl.program_id(0)
    size = cosine.shape[1]
    blocks = rows.shape[0] // BLOCK
    pre = dot_nn(rows[...], wq[...])
    pre_query[...] = pre
    gate[...] = dot_nn(rows[...], wu[...])
    for h in range(heads):
        part = slice(h * size, (h + 1) * size)
        q = rotate(swish(pre[:, part]), cosine[...], sine[...]).astype(BHALF)
        query[:, part] = q
        decay = decay_matrix(rate[step * heads + h])
        for b in range(blocks):
            span = slice(b * BLOCK, (b + 1) * BLOCK)
            weights = (dot_nt(q[span], keys[span, part]) * decay).astype(BHALF)
            intra[span, part] = dot_nn(weights, values[span, part])


def qu(rate, rows, wq, wu, cosine, sine, keys, values, steps):
    tokens, width = rows.shape
    heads = rate.shape[0]
    group = heads // steps
    cols = group * (width // heads)
    tile = lambda n: pl.BlockSpec((n, cols), lambda i: (0, i))
    whole = lambda a: pl.BlockSpec(a.shape, lambda i: (0, 0))
    return call(
        functools.partial(qu_body, group),
        (steps,),
        [SMEM_SPEC, whole(rows), tile(width), tile(width), whole(cosine), whole(sine)]
        + [tile(tokens)] * 2,
        [tile(tokens)] * 4,
        [shape_of(rows.shape, d) for d in (FLOAT, BHALF, FLOAT, FLOAT)],
        4 * tokens * width * width,
        20 * tokens * width + 4 * width * width,
    )(rate, rows, wq, wu, cosine, sine, keys, values)


def join_body(heads, use_next, rate, x, intra, query, gate, state, before, wo, *outs):
    attended, gated, resid, normed, used = outs
    size = state.shape[1]
    pieces = []
    for h in range(heads):
        part = slice(h * size, (h + 1) * size)
        own_rate = rate[h]
        here = state[h]
        if use_next:
            here = scaled_by(-BLOCK * own_rate, here) + before[h]
        here = here.astype(BHALF)
        used[h] = here
        q = (query[:, part].astype(FLOAT) * query_decay(own_rate, size)).astype(BHALF)
        pieces.append(intra[:, part] + dot_nn(q, here))
    full = jnp.concatenate(pieces, axis=1)
    attended[...] = full
    g = (srms(full) * gate[...]).astype(BHALF)
    gated[...] = g
    r = x[...].astype(FLOAT) + dot_nn(g, wo[...])
    resid[...] = r
    normed[...] = srms(r).astype(BHALF)


def join(block, rate, x, intra, query, gate, state, contrib, wo):
    width = x.shape[1]
    heads, size = state.shape[0], state.shape[1]
    before = contrib
    if block > 1:
        for b in range(block - 1):
            state = jnp.exp2(-BLOCK * rate)[:, None, None] * state + contrib[b]
    row = pl.BlockSpec((BLOCK, width), lambda i: (block, 0))
    out_row = pl.BlockSpec((BLOCK, width), lambda i: (0, 0))
    cube = pl.BlockSpec((heads, size, size), lambda i: (0, 0, 0))
    earlier = max(block - 1, 0)
    return call(
        functools.partial(join_body, heads, block > 0),
        (1,),
        [SMEM_SPEC, row, row, row, row, cube]
        + [pl.BlockSpec((None, heads, size, size), lambda i: (earlier, 0, 0, 0))]
        + [pl.BlockSpec(wo.shape, lambda i: (0, 0))],
        [out_row] * 4 + [cube],
        [shape_of((BLOCK, width), d) for d in (FLOAT, BHALF, FLOAT, BHALF)]
        + [shape_of((heads, size, size), BHALF)],
        2 * BLOCK * width * (width + size),
        24 * BLOCK * width + 2 * width * width,
    )(rate, x, intra, query, gate, state, before, wo)


def unit_body(n0, n1, c0, c1, gate_t, linear_t, down, keep, ship, hidden, gate_back, linear_back):
    rows = jnp.concatenate([n0[...], n1[...]], axis=0)
    cots = jnp.concatenate([c0[...], c1[...]], axis=0)
    gate = dot_nt(rows, gate_t[...])
    linear = dot_nt(rows, linear_t[...])
    inner = (gate * linear).astype(BHALF)
    hidden[...] = inner
    inner_cot = dot_nt(cots, down[...])
    gb = (inner_cot * linear).astype(BHALF)
    lb = (inner_cot * gate).astype(BHALF)
    gate_back[...] = gb
    linear_back[...] = lb
    feed = dot_nn(inner, down[...])
    cot = dot_nn(gb, gate_t[...]) + dot_nn(lb, linear_t[...])
    keep[0] = cot[:BLOCK]
    keep[1] = feed[:BLOCK]
    ship[0] = cot[BLOCK:].astype(BHALF)
    ship[1] = feed[BLOCK:].astype(BHALF)


def unit(block, rows, cots, gate_t, linear_t, down):
    width = rows[0].shape[1]
    inner = down.shape[0]
    piece = pl.BlockSpec((BLOCK, width), lambda i: (0, 0))
    cot = pl.BlockSpec((BLOCK, width), lambda i: (block, 0))
    whole = lambda s: pl.BlockSpec(s, lambda i: (0,) * len(s))
    wide = (2 * BLOCK, inner)
    pair = (2, BLOCK, width)
    return call(
        unit_body,
        (1,),
        [piece] * 2 + [cot] * 2 + [whole(down.shape)] * 3,
        [whole(pair)] * 2 + [whole(wide)] * 3,
        [shape_of(pair, FLOAT), shape_of(pair, BHALF)] + [shape_of(wide, BHALF)] * 3,
        24 * BLOCK * width * inner,
        6 * width * inner + 20 * BLOCK * width,
    )(*rows, *cots, gate_t, linear_t, down)


def place_in(order, count, shard, place):
    relative = jnp.bitwise_xor(shard, place)
    position = 0
    for mask in order:
        position = position * 2 + jnp.bitwise_and(relative // mask, 1)
    return position


def unit_grads_body(groups, orders, place, *refs):
    per = 2 + 2 + 3
    ins = refs[: groups * per]
    pair_out, down_out = refs[groups * per : groups * per + 2]
    rows, cots, hidden, gate_back, linear_back, sems = refs[groups * per + 2 :]
    copies = [[] for _ in range(groups)]
    for g in range(groups):
        n0, n1, c0, c1, h, gb, lb = ins[g * per : (g + 1) * per]
        block = g % 2
        span = pl.ds(block * BLOCK, BLOCK)
        moves = [
            (gb, gate_back.at[g]),
            (n0, rows.at[g, pl.ds(0, BLOCK)]),
            (n1, rows.at[g, pl.ds(BLOCK, BLOCK)]),
            (lb, linear_back.at[g]),
            (h, hidden.at[g]),
            (c0.at[span], cots.at[g, pl.ds(0, BLOCK)]),
            (c1.at[span], cots.at[g, pl.ds(BLOCK, BLOCK)]),
        ]
        for k, (source, target) in enumerate(moves):
            copies[g].append(pltpu.make_async_copy(source, target, sems.at[g, k]))
    for first, last in ((0, 3), (3, 4), (4, 7)):
        for g in range(groups):
            for copy in copies[g][first:last]:
                copy.start()
    count = pair_out.shape[0]
    here = place[0]

    def total(left, right, first, last):
        acc = None
        for g in range(groups):
            for copy in copies[g][first:last]:
                copy.wait()
            term = dot_tn(left[g], right[g])
            acc = term if acc is None else acc + term
        return acc

    def store(acc, put, order):
        size = acc.shape[1] // count
        for shard in range(count):
            put(place_in(order, count, shard, here), acc[:, shard * size : (shard + 1) * size])

    def put_pair(k):
        def put(position, value):
            pair_out[position, k] = value.astype(BHALF)
        return put

    def put_down(position, value):
        down_out[position] = value.astype(BHALF)

    store(total(gate_back, rows, 0, 3), put_pair(0), orders[0])
    store(total(linear_back, rows, 3, 4), put_pair(1), orders[0])
    store(total(hidden, cots, 4, 7), put_down, orders[1])


def unit_grads(place, groups, orders, count):
    inner = groups[0][4].shape[1]
    width = groups[0][0].shape[1]
    flat = [a for group in groups for a in group]
    any_spec = pl.BlockSpec(memory_space=pl.ANY)
    size = width // count
    pair = (count, 2, inner, size)
    single = (count, inner, size)
    n = len(groups)
    whole = lambda s: pl.BlockSpec(s, lambda i: (0,) * len(s))
    return call(
        functools.partial(unit_grads_body, n, orders),
        (1,),
        [SMEM_SPEC] + [any_spec] * len(flat),
        [whole(pair), whole(single)],
        [shape_of(pair, BHALF), shape_of(single, BHALF)],
        12 * n * BLOCK * width * inner,
        n * 2 * BLOCK * (4 * width + 6 * inner) + 6 * width * inner,
        scratch=[
            pltpu.VMEM((n, 2 * BLOCK, width), BHALF),
            pltpu.VMEM((n, 2 * BLOCK, width), BHALF),
            pltpu.VMEM((n, 2 * BLOCK, inner), BHALF),
            pltpu.VMEM((n, 2 * BLOCK, inner), BHALF),
            pltpu.VMEM((n, 2 * BLOCK, inner), BHALF),
            pltpu.SemaphoreType.DMA((n, 7)),
        ],
        vmem=VMEM_BYTES if n <= 4 else 2 * VMEM_BYTES,
    )(place, *flat)


def turn_body(heads, rate, keep, got, far, resid, cot, attended, gate, query, wo, *outs):
    resid_cot, branch, modulate, back, direct = outs
    size = direct.shape[1]
    normed_cot = keep[0] + got[0].astype(FLOAT)
    for k in range(far.shape[0]):
        normed_cot = normed_cot + far[k].astype(FLOAT)
    rc = cot[...].astype(FLOAT) + srms_back(resid[...], normed_cot)
    resid_cot[...] = rc
    bb = rc.astype(BHALF)
    branch[...] = bb
    gated_cot = dot_nt(bb, wo[...])
    att = attended[...]
    modulate[...] = (gated_cot * srms(att)).astype(BHALF)
    ab = srms_back(att, gated_cot * gate[...]).astype(BHALF)
    back[...] = ab
    for h in range(heads):
        part = slice(h * size, (h + 1) * size)
        q = (query[:, part].astype(FLOAT) * query_decay(rate[h], size)).astype(BHALF)
        direct[h] = dot_tn(q, ab[:, part])


def turn(block, rate, keep, got, far, resid, cot, attended, gate, query, wo):
    width = resid.shape[1]
    heads = rate.shape[0]
    size = width // heads
    row = pl.BlockSpec((BLOCK, width), lambda i: (block, 0))
    own = pl.BlockSpec((BLOCK, width), lambda i: (0, 0))
    first = pl.BlockSpec((1, BLOCK, width), lambda i: (0, 0, 0))
    cube = pl.BlockSpec((heads, size, size), lambda i: (0, 0, 0))
    return call(
        functools.partial(turn_body, heads),
        (1,),
        [SMEM_SPEC, first, first, pl.BlockSpec(far.shape, lambda i: (0, 0, 0)), own, row, own]
        + [row, row, pl.BlockSpec(wo.shape, lambda i: (0, 0))],
        [own] * 4 + [cube],
        [shape_of((BLOCK, width), d) for d in (FLOAT, BHALF, BHALF, BHALF)]
        + [shape_of((heads, size, size), FLOAT)],
        2 * BLOCK * width * (width + size),
        32 * BLOCK * width + 2 * width * width,
    )(rate, keep, got, far, resid, cot, attended, gate, query, wo)


def query_body(heads, blocks, rate, pre_query, query, keys, values, cosine, sine, *refs):
    backs = refs[:blocks]
    used = refs[blocks : 2 * blocks]
    query_back, key_part, value_part = refs[2 * blocks :]
    step = pl.program_id(0)
    size = cosine.shape[1]
    for h in range(heads):
        part = slice(h * size, (h + 1) * size)
        own_rate = rate[step * heads + h]
        decay = decay_matrix(own_rate)
        row = query_decay(own_rate, size)
        for b in range(blocks):
            span = slice(b * BLOCK, (b + 1) * BLOCK)
            q, k, v = query[span, part], keys[span, part], values[span, part]
            ab = backs[b][:, part]
            weights = (dot_nt(q, k) * decay).astype(BHALF)
            weights_back = (dot_nt(ab, v) * decay).astype(BHALF)
            value_part[span, part] = dot_tn(weights, ab)
            key_part[span, part] = dot_tn(weights_back, q)
            cot = dot_nn(weights_back, k) + row * dot_nt(ab, used[b][h])
            cot = unrotate(cot, cosine[span], sine[span])
            query_back[span, part] = (cot * swish_slope(pre_query[span, part])).astype(BHALF)


def query_side(rate, pre_query, query, keys, values, cosine, sine, backs, used, steps):
    tokens, width = query.shape
    heads = rate.shape[0]
    size = width // heads
    group = heads // steps
    cols = group * size
    blocks = len(backs)
    tile = pl.BlockSpec((tokens, cols), lambda i: (0, i))
    whole = lambda a: pl.BlockSpec(a.shape, lambda i: (0, 0))
    return call(
        functools.partial(query_body, group, blocks),
        (steps,),
        [SMEM_SPEC] + [tile] * 4 + [whole(cosine), whole(sine)]
        + [pl.BlockSpec((BLOCK, cols), lambda i: (0, i))] * blocks
        + [pl.BlockSpec((group, size, size), lambda i: (i, 0, 0))] * blocks,
        [tile] * 3,
        [shape_of(query.shape, d) for d in (BHALF, FLOAT, FLOAT)],
        12 * tokens * width * BLOCK,
        24 * tokens * width,
    )(rate, pre_query, query, keys, values, cosine, sine, *backs, *used)


def key_body(heads, blocks, rate, pre_key, keys, values, key_part, value_part, *refs):
    cosine, sine, state = refs[:3]
    direct = refs[3 : 3 + blocks]
    key_back, value_back = refs[3 + blocks :]
    step = pl.program_id(0)
    size = cosine.shape[1]
    for h in range(heads):
        part = slice(h * size, (h + 1) * size)
        own_rate = rate[step * heads + h]
        decay = key_decay(own_rate, size)
        here = state[h]
        for b in reversed(range(blocks)):
            span = slice(b * BLOCK, (b + 1) * BLOCK)
            used = here.astype(BHALF)
            cot = key_part[span, part] + decay * dot_nt(values[span, part], used)
            decayed = (keys[span, part].astype(FLOAT) * decay).astype(BHALF)
            vcot = value_part[span, part] + dot_nn(decayed, used)
            cot = unrotate(cot, cosine[span], sine[span])
            key_back[span, part] = (cot * swish_slope(pre_key[span, part])).astype(BHALF)
            value_back[span, part] = vcot.astype(BHALF)
            if b:
                here = scaled_by(-BLOCK * own_rate, here) + direct[b][h]


def key_side(rate, pre_key, keys, values, key_part, value_part, cosine, sine, state, direct, steps):
    tokens, width = keys.shape
    heads = rate.shape[0]
    size = width // heads
    group = heads // steps
    cols = group * size
    blocks = len(direct)
    tile = pl.BlockSpec((tokens, cols), lambda i: (0, i))
    whole = lambda a: pl.BlockSpec(a.shape, lambda i: (0, 0))
    cube = pl.BlockSpec((group, size, size), lambda i: (i, 0, 0))
    return call(
        functools.partial(key_body, group, blocks),
        (steps,),
        [SMEM_SPEC] + [tile] * 5 + [whole(cosine), whole(sine), cube] + [cube] * blocks,
        [tile] * 2,
        [shape_of(keys.shape, BHALF)] * 2,
        4 * tokens * width * size,
        20 * tokens * width,
    )(rate, pre_key, keys, values, key_part, value_part, cosine, sine, state, *direct)


def grads_body(lefts, pairs, core, *refs):
    left = refs[:lefts]
    right = refs[lefts:-1]
    out = refs[-1]
    for k, (l, rs) in enumerate(pairs):
        acc = None
        start = 0
        for piece in rs:
            r = right[piece]
            rows = r.shape[0]
            term = dot_tn(left[l][start : start + rows], r[...])
            start += rows
            acc = term if acc is None else acc + term
        out[0, k] = acc.astype(BHALF)


def grads(core, lefts, rights, pairs):
    tokens, width = lefts[0].shape
    cols = rights[0].shape[1]
    half = width // 2
    spec = pltpu.PrefetchScalarGridSpec(
        num_scalar_prefetch=1,
        grid=(2,),
        in_specs=[pl.BlockSpec((tokens, half), lambda i, c: (0, i ^ c[0]))] * len(lefts)
        + [pl.BlockSpec(r.shape, lambda i, c: (0, 0)) for r in rights],
        out_specs=pl.BlockSpec((1, len(pairs), half, cols), lambda i, c: (i, 0, 0, 0)),
    )
    n = len(pairs)
    body = functools.partial(grads_body, len(lefts), pairs)
    return pl.pallas_call(
        body,
        grid_spec=spec,
        out_shape=shape_of((2, n, half, cols), BHALF),
        cost_estimate=pl.CostEstimate(
            flops=2 * n * tokens * width * cols, bytes_accessed=4 * n * width * cols, transcendentals=0
        ),
        compiler_params=pltpu.CompilerParams(vmem_limit_bytes=VMEM_BYTES),
    )(core, *lefts, *rights)


def tokens_body(x, rc, qb, kb, vb, mb, wq, wk, wv, wm, out):
    grad = dot_nt(qb[...], wq[...]) + dot_nt(kb[...], wk[...])
    grad = grad + dot_nt(vb[...], wv[...]) + dot_nt(mb[...], wm[...])
    out[...] = rc[...] + srms_back(x[...].astype(FLOAT), grad)


def tokens_side(block, x, rc, qb, kb, vb, mb, weights):
    tokens, width = x.shape
    row = pl.BlockSpec((BLOCK, width), lambda i: (block, 0))
    own = pl.BlockSpec((BLOCK, width), lambda i: (0, 0))
    whole = pl.BlockSpec((width, width), lambda i: (0, 0))
    return call(
        tokens_body,
        (1,),
        [row, own, row, row, row, own] + [whole] * 4,
        own,
        shape_of((BLOCK, width), FLOAT),
        8 * BLOCK * width * width,
        8 * width * width + 20 * BLOCK * width,
    )(x, rc, qb, kb, vb, mb, *weights)


def angle_tables(position, halves):
    column = jnp.arange(halves, dtype=jnp.int32)
    factor = 1 + jnp.right_shift(jnp.full((halves,), 16384, jnp.int32), column // 4)
    phase = position[:, None] * factor[None, :] % 65536
    turned = phase.astype(FLOAT) * (2.0 * math.pi / 65536.0)
    cosine, sine = jnp.cos(turned), jnp.sin(turned)
    return jnp.concatenate([cosine, cosine], 1), jnp.concatenate([-sine, sine], 1)


def shards(
    tokens,
    query_weight,
    key_weight,
    value_weight,
    modulate_weight,
    output_weight,
    gate_weight,
    linear_weight,
    down_weight,
    cotangent,
    decay_exponent,
):
    count, width = tokens.shape
    heads = decay_exponent.shape[0]
    size = width // heads
    runs, members = lax.axis_size("seq"), lax.axis_size("tp")
    devices = runs * members
    length = min(SEQ_LEN, count * devices)
    span = length // count
    blocks = count // BLOCK
    seq_place = lax.axis_index("seq")
    place = seq_place * members + lax.axis_index("tp")
    core = bit_of(place, 1).astype(jnp.int32).reshape(1)
    position = (place * count + jnp.arange(count, dtype=jnp.int32)) % length
    rate = jnp.exp2(-decay_exponent.astype(FLOAT))
    cosine, sine = angle_tables(position, size // 2)
    ring = bits_of(members)
    far = ring[1:]

    normed, pre_key, keys, values, contrib, local = kv(
        rate, tokens, key_weight, value_weight, cosine, sine, 1
    )
    state, mark = decayed_scan(local, rate, float(count), span, place, False)
    pre_query, query, gate, intra = qu(
        rate, normed, query_weight, modulate_weight, cosine, sine, keys, values, 2
    )
    cots = gather_group(after(cotangent, mark), far + [1])
    joined = [
        join(b, rate, tokens, intra, query, gate, state, contrib, output_weight)
        for b in range(blocks)
    ]

    gate_t, linear_t = gate_weight.T, linear_weight.T
    gathered = [gather_group(joined[b][3], far + [1]) for b in range(blocks)]
    results = {}
    for r in range(0, members, 2):
        for b in range(blocks):
            results[r, b] = unit(
                b, gathered[b][r : r + 2], cots[r : r + 2], gate_t, linear_t, down_weight
            )
    groups = [
        tuple(gathered[b][r : r + 2]) + tuple(cots[r : r + 2]) + tuple(results[r, b][2:])
        for r in range(0, members, 2)
        for b in range(blocks)
    ]
    near = {}
    for key, value in results.items():
        near[key] = (value[0], swap(value[1], 1))
    arrived = {}
    for part in range(2):
        for b in range(blocks):
            rows = {
                r: near[r, b][0][part] + near[r, b][1][part].astype(FLOAT)
                for r in range(2, members, 2)
            }
            got = []
            for mask in reversed(far):
                for r in [r for r in rows if r & mask]:
                    value = swap(rows.pop(r).astype(BHALF), mask)
                    if r == mask:
                        got.append(value)
                    else:
                        rows[r ^ mask] = rows[r ^ mask] + value.astype(FLOAT)
            arrived[b, part] = got

    turned = [
        turn(
            b, rate, near[0, b][0], near[0, b][1], jnp.stack(arrived[b, 0]), joined[b][2],
            cotangent, joined[b][0], gate, query, output_weight,
        )
        for b in range(blocks)
    ]
    line = bits_of(runs)
    across = max(members // 2, 1)
    orders = (line, [m for m in line if m >= across] + [m for m in line if m < across])
    seq_scalar = seq_place.astype(jnp.int32).reshape(1)
    pair_part, down_part = unit_grads(seq_scalar, groups, orders, runs)

    decays = jnp.exp2(-BLOCK * rate)[:, None, None]
    inbound = turned[blocks - 1][4]
    for b in reversed(range(blocks - 1)):
        inbound = decays * inbound + turned[b][4]
    outer, _ = decayed_scan(inbound, rate, float(count), span, place, True)
    backs = [t[3] for t in turned]
    query_back, key_part, value_part = query_side(
        rate, pre_query, query, keys, values, cosine, sine, backs, [j[4] for j in joined], 2
    )
    rest = bits_of(devices)[1:]
    lines = [
        [m for m in rest if m < members],
        [m for m in rest if members <= m < members * across],
        [m for m in rest if m >= members * across],
    ]

    def order_of(k):
        return [m for i in range(3) for m in lines[(i + k) % 3]]

    def chip_sums(part):
        kept = (part[0].astype(FLOAT) + swap(part[1], 1).astype(FLOAT)).astype(BHALF)
        return [kept[k] for k in range(kept.shape[0])]

    def rest_of(piece, k, done):
        order = order_of(k)
        piece = double(halve(piece, order[done:], place), list(reversed(order)), place)
        return double(piece, [1], place).astype(FLOAT)

    gated = jnp.concatenate([j[1] for j in joined], axis=0)
    early = grads(
        core,
        [gated, normed],
        [t[1] for t in turned] + [t[2] for t in turned] + [query_back],
        [
            (0, list(range(blocks))),
            (1, list(range(blocks, 2 * blocks))),
            (1, [2 * blocks]),
        ],
    )
    moved = [halve(piece, order_of(k)[:1], place) for k, piece in enumerate(chip_sums(early))]
    key_back, value_back = key_side(
        rate, pre_key, keys, values, key_part, value_part, cosine, sine, outer,
        [t[4] for t in turned], 1,
    )
    late = grads(core, [normed], [key_back, value_back], [(0, [0]), (0, [1])])
    weights = (query_weight, key_weight, value_weight, modulate_weight)
    late_sums = chip_sums(late)
    late_moved = [halve(p, order_of(k)[:1], place) for k, p in enumerate(late_sums)]
    late_key = after(key_back, *late_sums)
    tokens_grad = jnp.concatenate(
        [
            tokens_side(
                b, tokens, turned[b][0], query_back, late_key, value_back, turned[b][2], weights
            )
            for b in range(blocks)
        ],
        axis=0,
    )

    mixed = jnp.concatenate(
        [
            (
                joined[b][2] + near[0, b][0][1] + near[0, b][1][1].astype(FLOAT)
                + sum(a.astype(FLOAT) for a in arrived[b, 1])
            ).astype(BHALF)
            for b in range(blocks)
        ],
        axis=0,
    )
    masks = [[members * m for m in order] for order in orders]
    pair_grad = fold(pair_part, masks[0]).astype(FLOAT)
    down_grad = fold(down_part, masks[1]).astype(FLOAT)
    gate_grad, linear_grad = pair_grad[0].T, pair_grad[1].T

    output_grad, modulate_grad, query_grad = [rest_of(p, k, 1) for k, p in enumerate(moved)]
    key_grad, value_grad = [rest_of(p, k, 1) for k, p in enumerate(late_moved)]
    return (
        mixed,
        tokens_grad,
        query_grad,
        key_grad,
        value_grad,
        modulate_grad,
        output_grad,
        gate_grad,
        linear_grad,
        down_grad,
    )


def solution(mesh):
    return jax.shard_map(
        shards,
        mesh=mesh,
        in_specs=(
            P(("seq", "tp"), None),
            P(),
            P(),
            P(),
            P(),
            P(),
            P(None, "tp"),
            P(None, "tp"),
            P("tp", None),
            P(("seq", "tp"), None),
            P(),
        ),
        out_specs=(
            P(("seq", "tp"), None),
            P(("seq", "tp"), None),
            P(),
            P(),
            P(),
            P(),
            P(),
            P("seq", "tp"),
            P("seq", "tp"),
            P("tp", "seq"),
        ),
        check_vma=False,
    )
```

```python
import functools
import math

import jax
import jax.numpy as jnp
from jax import lax
from jax.experimental import pallas as pl
from jax.experimental.pallas import tpu as pltpu
from jax.sharding import PartitionSpec as P

BLOCK = 256
SEQ_LEN = 16384
EPS = 1e-06
FLOAT = jnp.float32
BHALF = jnp.bfloat16
VMEM_BYTES = 24 * 1024 * 1024


def bits_of(count):
    return [1 << b for b in range(count.bit_length() - 1)]


def swap(value, mask, axes=("seq", "tp")):
    count = lax.axis_size(axes)
    return lax.ppermute(value, axes, [(s, s ^ mask) for s in range(count)])


def bit_of(place, mask):
    return (place // mask) % 2


def after(value, *others):
    return lax.optimization_barrier((value,) + others)[0]


def halve(value, masks, place):
    for mask in masks:
        halves = value.reshape((2, value.shape[0] // 2) + value.shape[1:])
        bit = bit_of(place, mask)
        keep = lax.dynamic_index_in_dim(halves, bit, 0, False)
        send = lax.dynamic_index_in_dim(halves, 1 - bit, 0, False)
        value = (keep.astype(FLOAT) + swap(send, mask).astype(FLOAT)).astype(BHALF)
    return value


def double(value, masks, place):
    for mask in masks:
        other = swap(value, mask)
        bit = bit_of(place, mask)
        first = jnp.where(bit == 0, value, other)
        second = jnp.where(bit == 0, other, value)
        value = jnp.concatenate([first, second], axis=0)
    return value


def fold(value, masks):
    for mask in masks:
        half = value.shape[0] // 2
        got = swap(value[half:], mask)
        value = (value[:half].astype(FLOAT) + got.astype(FLOAT)).astype(BHALF)
    return value[0]


def decayed_scan(state, rate, unit, span, place, reverse):
    heads = state.shape[0]
    half = heads // 2
    bit = bit_of(place, 1)
    halves = state.reshape((2, half) + state.shape[1:])
    mine = lax.dynamic_index_in_dim(halves, bit, 0, False)
    theirs = lax.dynamic_index_in_dim(halves, 1 - bit, 0, False)
    other = swap(theirs.astype(BHALF), 1).astype(FLOAT)
    own_rate = lax.dynamic_index_in_dim(rate.reshape(2, half), bit, 0, False)

    def power(count):
        return jnp.exp2(-unit * count * own_rate)[:, None, None]

    later = 1 - bit if reverse else bit
    core_later = jnp.where(later == 1, mine, other)
    core_first = jnp.where(later == 1, other, mine)
    total = power(1.0) * core_first + core_later
    prefix = jnp.zeros_like(total)
    mark = None
    for mask in bits_of(span)[1:]:
        bit = bit_of(place, mask)
        later = 1 - bit if reverse else bit
        sent = swap(total.astype(BHALF), mask)
        mark = sent if mark is None else mark
        got = sent.astype(FLOAT)
        within = (place % mask) // 2
        if reverse:
            within = mask // 2 - 1 - within
        scale = power(2.0 * within.astype(FLOAT))
        prefix = prefix + jnp.where(later == 1, scale * got, 0.0)
        low = jnp.where(later == 1, got, total)
        high = jnp.where(later == 1, total, got)
        total = power(float(mask)) * low + high
    second_pre = power(1.0) * prefix + core_first
    bit = bit_of(place, 1)
    later = 1 - bit if reverse else bit
    own = jnp.where(later == 1, second_pre, prefix)
    away = jnp.where(later == 1, prefix, second_pre)
    got = swap(away.astype(BHALF), 1).astype(FLOAT)
    first = jnp.where(bit == 0, own, got)
    second = jnp.where(bit == 0, got, own)
    return jnp.concatenate([first, second], axis=0), mark


def gather_group(value, masks):
    rows = {0: value}
    for mask in masks:
        for r in list(rows):
            rows[r | mask] = swap(rows[r], mask)
    return [rows[r] for r in range(len(rows))]


def dot_nn(left, right):
    return jnp.dot(left, right, preferred_element_type=FLOAT)


def dot_tn(left, right):
    return lax.dot_general(left, right, (((0,), (0,)), ((), ())), preferred_element_type=FLOAT)


def dot_nt(left, right):
    return lax.dot_general(left, right, (((1,), (1,)), ((), ())), preferred_element_type=FLOAT)


def srms(values):
    return values * lax.rsqrt(jnp.mean(values * values, axis=-1, keepdims=True) + EPS)


def srms_back(values, gradient):
    scaled = lax.rsqrt(jnp.mean(values * values, axis=-1, keepdims=True) + EPS)
    normed = values * scaled
    return scaled * (gradient - normed * jnp.mean(gradient * normed, axis=-1, keepdims=True))


def swish(values):
    return values * jax.nn.sigmoid(values)


def swish_slope(values):
    sigmoid = jax.nn.sigmoid(values)
    return sigmoid * (1.0 + values * (1.0 - sigmoid))


def half_turn(values):
    return pltpu.roll(values, values.shape[-1] // 2, 1)


def rotate(values, cosine, sine):
    return values * cosine + half_turn(values) * sine


def unrotate(values, cosine, sine):
    return values * cosine - half_turn(values) * sine


def row_decay(rate, size, start, sign):
    offset = lax.broadcasted_iota(jnp.int32, (BLOCK, size), 0).astype(FLOAT)
    return jnp.exp2(-(start + sign * offset) * rate)


def query_decay(rate, size):
    return row_decay(rate, size, 1.0, 1.0)


def key_decay(rate, size):
    return row_decay(rate, size, BLOCK - 1.0, -1.0)


def decay_matrix(rate):
    row = lax.broadcasted_iota(jnp.int32, (BLOCK, BLOCK), 0)
    column = lax.broadcasted_iota(jnp.int32, (BLOCK, BLOCK), 1)
    distance = (row - column).astype(FLOAT)
    return jnp.where(distance >= 0.0, jnp.exp2(-jnp.maximum(distance, 0.0) * rate), 0.0)


def scaled_by(factor_exponent, values):
    return jnp.exp2(jnp.full(values.shape, factor_exponent, FLOAT)) * values


def shape_of(shape, dtype):
    return jax.ShapeDtypeStruct(shape, dtype)


SMEM_SPEC = pl.BlockSpec(memory_space=pltpu.SMEM)


def call(body, grid, in_specs, out_specs, out_shape, flops, moved, scratch=(), vmem=VMEM_BYTES):
    return pl.pallas_call(
        body,
        grid=grid,
        in_specs=in_specs,
        out_specs=out_specs,
        out_shape=out_shape,
        scratch_shapes=scratch,
        cost_estimate=pl.CostEstimate(flops=flops, bytes_accessed=moved, transcendentals=0),
        compiler_params=pltpu.CompilerParams(vmem_limit_bytes=vmem),
    )


def kv_body(heads, rate, x, wk, wv, cosine, sine, normed, pre_key, keys, values, contrib, local):
    step = pl.program_id(0)
    size = cosine.shape[1]
    blocks = x.shape[0] // BLOCK

    @pl.when(step == 0)
    def _():
        normed[...] = srms(x[...].astype(FLOAT)).astype(BHALF)

    rows = normed[...]
    pre = dot_nn(rows, wk[...])
    pre_key[...] = pre
    val = dot_nn(rows, wv[...]).astype(BHALF)
    values[...] = val
    for h in range(heads):
        part = slice(h * size, (h + 1) * size)
        own_rate = rate[step * heads + h]
        key = rotate(swish(pre[:, part]), cosine[...], sine[...]).astype(BHALF)
        keys[:, part] = key
        decay = key_decay(own_rate, size)
        total = None
        for b in range(blocks):
            span = slice(b * BLOCK, (b + 1) * BLOCK)
            decayed = (key[span].astype(FLOAT) * decay).astype(BHALF)
            state = dot_tn(decayed, val[span, part])
            contrib[b, h] = state
            total = state if total is None else scaled_by(-BLOCK * own_rate, total) + state
        local[h] = total


def kv(rate, x, wk, wv, cosine, sine, steps):
    tokens, width = x.shape
    heads = rate.shape[0]
    size = width // heads
    group = heads // steps
    cols = group * size
    blocks = tokens // BLOCK
    tile = lambda n: pl.BlockSpec((n, cols), lambda i: (0, i))
    whole = lambda a: pl.BlockSpec(a.shape, lambda i: (0, 0))
    return call(
        functools.partial(kv_body, group),
        (steps,),
        [SMEM_SPEC, whole(x), tile(width), tile(width), whole(cosine), whole(sine)],
        [
            whole(x),
            tile(tokens),
            tile(tokens),
            tile(tokens),
            pl.BlockSpec((blocks, group, size, size), lambda i: (0, i, 0, 0)),
            pl.BlockSpec((group, size, size), lambda i: (i, 0, 0)),
        ],
        [
            shape_of(x.shape, BHALF),
            shape_of(x.shape, FLOAT),
            shape_of(x.shape, BHALF),
            shape_of(x.shape, BHALF),
            shape_of((blocks, heads, size, size), FLOAT),
            shape_of((heads, size, size), FLOAT),
        ],
        4 * tokens * width * width,
        12 * tokens * width + 4 * width * width,
    )(rate, x, wk, wv, cosine, sine)


def qu_body(heads, rate, rows, wq, wu, cosine, sine, keys, values, pre_query, query, gate, intra):
    step = pl.program_id(0)
    size = cosine.shape[1]
    blocks = rows.shape[0] // BLOCK
    pre = dot_nn(rows[...], wq[...])
    pre_query[...] = pre
    gate[...] = dot_nn(rows[...], wu[...])
    for h in range(heads):
        part = slice(h * size, (h + 1) * size)
        q = rotate(swish(pre[:, part]), cosine[...], sine[...]).astype(BHALF)
        query[:, part] = q
        decay = decay_matrix(rate[step * heads + h])
        for b in range(blocks):
            span = slice(b * BLOCK, (b + 1) * BLOCK)
            weights = (dot_nt(q[span], keys[span, part]) * decay).astype(BHALF)
            intra[span, part] = dot_nn(weights, values[span, part])


def qu(rate, rows, wq, wu, cosine, sine, keys, values, steps):
    tokens, width = rows.shape
    heads = rate.shape[0]
    group = heads // steps
    cols = group * (width // heads)
    tile = lambda n: pl.BlockSpec((n, cols), lambda i: (0, i))
    whole = lambda a: pl.BlockSpec(a.shape, lambda i: (0, 0))
    return call(
        functools.partial(qu_body, group),
        (steps,),
        [SMEM_SPEC, whole(rows), tile(width), tile(width), whole(cosine), whole(sine)]
        + [tile(tokens)] * 2,
        [tile(tokens)] * 4,
        [shape_of(rows.shape, d) for d in (FLOAT, BHALF, FLOAT, FLOAT)],
        4 * tokens * width * width,
        20 * tokens * width + 4 * width * width,
    )(rate, rows, wq, wu, cosine, sine, keys, values)


def join_body(heads, use_next, rate, x, intra, query, gate, state, before, wo, *outs):
    attended, gated, resid, normed, used = outs
    size = state.shape[1]
    pieces = []
    for h in range(heads):
        part = slice(h * size, (h + 1) * size)
        own_rate = rate[h]
        here = state[h]
        if use_next:
            here = scaled_by(-BLOCK * own_rate, here) + before[h]
        here = here.astype(BHALF)
        used[h] = here
        q = (query[:, part].astype(FLOAT) * query_decay(own_rate, size)).astype(BHALF)
        pieces.append(intra[:, part] + dot_nn(q, here))
    full = jnp.concatenate(pieces, axis=1)
    attended[...] = full
    g = (srms(full) * gate[...]).astype(BHALF)
    gated[...] = g
    r = x[...].astype(FLOAT) + dot_nn(g, wo[...])
    resid[...] = r
    normed[...] = srms(r).astype(BHALF)


def join(block, rate, x, intra, query, gate, state, contrib, wo):
    width = x.shape[1]
    heads, size = state.shape[0], state.shape[1]
    before = contrib
    if block > 1:
        for b in range(block - 1):
            state = jnp.exp2(-BLOCK * rate)[:, None, None] * state + contrib[b]
    row = pl.BlockSpec((BLOCK, width), lambda i: (block, 0))
    out_row = pl.BlockSpec((BLOCK, width), lambda i: (0, 0))
    cube = pl.BlockSpec((heads, size, size), lambda i: (0, 0, 0))
    earlier = max(block - 1, 0)
    return call(
        functools.partial(join_body, heads, block > 0),
        (1,),
        [SMEM_SPEC, row, row, row, row, cube]
        + [pl.BlockSpec((None, heads, size, size), lambda i: (earlier, 0, 0, 0))]
        + [pl.BlockSpec(wo.shape, lambda i: (0, 0))],
        [out_row] * 4 + [cube],
        [shape_of((BLOCK, width), d) for d in (FLOAT, BHALF, FLOAT, BHALF)]
        + [shape_of((heads, size, size), BHALF)],
        2 * BLOCK * width * (width + size),
        24 * BLOCK * width + 2 * width * width,
    )(rate, x, intra, query, gate, state, before, wo)


def unit_body(n0, n1, c0, c1, gate_t, linear_t, down, keep, ship, hidden, gate_back, linear_back):
    rows = jnp.concatenate([n0[...], n1[...]], axis=0)
    cots = jnp.concatenate([c0[...], c1[...]], axis=0)
    gate = dot_nt(rows, gate_t[...])
    linear = dot_nt(rows, linear_t[...])
    inner = (gate * linear).astype(BHALF)
    hidden[...] = inner
    inner_cot = dot_nt(cots, down[...])
    gb = (inner_cot * linear).astype(BHALF)
    lb = (inner_cot * gate).astype(BHALF)
    gate_back[...] = gb
    linear_back[...] = lb
    feed = dot_nn(inner, down[...])
    cot = dot_nn(gb, gate_t[...]) + dot_nn(lb, linear_t[...])
    keep[0] = cot[:BLOCK]
    keep[1] = feed[:BLOCK]
    ship[0] = cot[BLOCK:].astype(BHALF)
    ship[1] = feed[BLOCK:].astype(BHALF)


def unit(block, rows, cots, gate_t, linear_t, down):
    width = rows[0].shape[1]
    inner = down.shape[0]
    piece = pl.BlockSpec((BLOCK, width), lambda i: (0, 0))
    cot = pl.BlockSpec((BLOCK, width), lambda i: (block, 0))
    whole = lambda s: pl.BlockSpec(s, lambda i: (0,) * len(s))
    wide = (2 * BLOCK, inner)
    pair = (2, BLOCK, width)
    return call(
        unit_body,
        (1,),
        [piece] * 2 + [cot] * 2 + [whole(down.shape)] * 3,
        [whole(pair)] * 2 + [whole(wide)] * 3,
        [shape_of(pair, FLOAT), shape_of(pair, BHALF)] + [shape_of(wide, BHALF)] * 3,
        24 * BLOCK * width * inner,
        6 * width * inner + 20 * BLOCK * width,
    )(*rows, *cots, gate_t, linear_t, down)


def place_in(order, count, shard, place):
    relative = jnp.bitwise_xor(shard, place)
    position = 0
    for mask in order:
        position = position * 2 + jnp.bitwise_and(relative // mask, 1)
    return position


def unit_grads_body(groups, orders, place, *refs):
    per = 2 + 2 + 3
    ins = refs[: groups * per]
    pair_out, down_out = refs[groups * per : groups * per + 2]
    rows, cots, hidden, gate_back, linear_back, sems = refs[groups * per + 2 :]
    copies = [[] for _ in range(groups)]
    for g in range(groups):
        n0, n1, c0, c1, h, gb, lb = ins[g * per : (g + 1) * per]
        block = g % 2
        span = pl.ds(block * BLOCK, BLOCK)
        moves = [
            (gb, gate_back.at[g]),
            (n0, rows.at[g, pl.ds(0, BLOCK)]),
            (n1, rows.at[g, pl.ds(BLOCK, BLOCK)]),
            (lb, linear_back.at[g]),
            (h, hidden.at[g]),
            (c0.at[span], cots.at[g, pl.ds(0, BLOCK)]),
            (c1.at[span], cots.at[g, pl.ds(BLOCK, BLOCK)]),
        ]
        for k, (source, target) in enumerate(moves):
            copies[g].append(pltpu.make_async_copy(source, target, sems.at[g, k]))
    for first, last in ((0, 3), (3, 4), (4, 7)):
        for g in range(groups):
            for copy in copies[g][first:last]:
                copy.start()
    count = pair_out.shape[0]
    here = place[0]

    def total(left, right, first, last):
        acc = None
        for g in range(groups):
            for copy in copies[g][first:last]:
                copy.wait()
            term = dot_tn(left[g], right[g])
            acc = term if acc is None else acc + term
        return acc

    def store(acc, put, order):
        size = acc.shape[1] // count
        for shard in range(count):
            put(place_in(order, count, shard, here), acc[:, shard * size : (shard + 1) * size])

    def put_pair(k):
        def put(position, value):
            pair_out[position, k] = value.astype(BHALF)
        return put

    def put_down(position, value):
        down_out[position] = value.astype(BHALF)

    store(total(gate_back, rows, 0, 3), put_pair(0), orders[0])
    store(total(linear_back, rows, 3, 4), put_pair(1), orders[0])
    store(total(hidden, cots, 4, 7), put_down, orders[1])


def unit_grads(place, groups, orders, count):
    inner = groups[0][4].shape[1]
    width = groups[0][0].shape[1]
    flat = [a for group in groups for a in group]
    any_spec = pl.BlockSpec(memory_space=pl.ANY)
    size = width // count
    pair = (count, 2, inner, size)
    single = (count, inner, size)
    n = len(groups)
    whole = lambda s: pl.BlockSpec(s, lambda i: (0,) * len(s))
    return call(
        functools.partial(unit_grads_body, n, orders),
        (1,),
        [SMEM_SPEC] + [any_spec] * len(flat),
        [whole(pair), whole(single)],
        [shape_of(pair, BHALF), shape_of(single, BHALF)],
        12 * n * BLOCK * width * inner,
        n * 2 * BLOCK * (4 * width + 6 * inner) + 6 * width * inner,
        scratch=[
            pltpu.VMEM((n, 2 * BLOCK, width), BHALF),
            pltpu.VMEM((n, 2 * BLOCK, width), BHALF),
            pltpu.VMEM((n, 2 * BLOCK, inner), BHALF),
            pltpu.VMEM((n, 2 * BLOCK, inner), BHALF),
            pltpu.VMEM((n, 2 * BLOCK, inner), BHALF),
            pltpu.SemaphoreType.DMA((n, 7)),
        ],
        vmem=VMEM_BYTES if n <= 4 else 2 * VMEM_BYTES,
    )(place, *flat)


def turn_body(heads, rate, keep, got, far, resid, cot, attended, gate, query, wo, *outs):
    resid_cot, branch, modulate, back, direct = outs
    size = direct.shape[1]
    normed_cot = keep[0] + got[0].astype(FLOAT)
    for k in range(far.shape[0]):
        normed_cot = normed_cot + far[k].astype(FLOAT)
    rc = cot[...].astype(FLOAT) + srms_back(resid[...], normed_cot)
    resid_cot[...] = rc
    bb = rc.astype(BHALF)
    branch[...] = bb
    gated_cot = dot_nt(bb, wo[...])
    att = attended[...]
    modulate[...] = (gated_cot * srms(att)).astype(BHALF)
    ab = srms_back(att, gated_cot * gate[...]).astype(BHALF)
    back[...] = ab
    for h in range(heads):
        part = slice(h * size, (h + 1) * size)
        q = (query[:, part].astype(FLOAT) * query_decay(rate[h], size)).astype(BHALF)
        direct[h] = dot_tn(q, ab[:, part])


def turn(block, rate, keep, got, far, resid, cot, attended, gate, query, wo):
    width = resid.shape[1]
    heads = rate.shape[0]
    size = width // heads
    row = pl.BlockSpec((BLOCK, width), lambda i: (block, 0))
    own = pl.BlockSpec((BLOCK, width), lambda i: (0, 0))
    first = pl.BlockSpec((1, BLOCK, width), lambda i: (0, 0, 0))
    cube = pl.BlockSpec((heads, size, size), lambda i: (0, 0, 0))
    return call(
        functools.partial(turn_body, heads),
        (1,),
        [SMEM_SPEC, first, first, pl.BlockSpec(far.shape, lambda i: (0, 0, 0)), own, row, own]
        + [row, row, pl.BlockSpec(wo.shape, lambda i: (0, 0))],
        [own] * 4 + [cube],
        [shape_of((BLOCK, width), d) for d in (FLOAT, BHALF, BHALF, BHALF)]
        + [shape_of((heads, size, size), FLOAT)],
        2 * BLOCK * width * (width + size),
        32 * BLOCK * width + 2 * width * width,
    )(rate, keep, got, far, resid, cot, attended, gate, query, wo)


def query_body(heads, blocks, rate, pre_query, query, keys, values, cosine, sine, *refs):
    backs = refs[:blocks]
    used = refs[blocks : 2 * blocks]
    query_back, key_part, value_part = refs[2 * blocks :]
    step = pl.program_id(0)
    size = cosine.shape[1]
    for h in range(heads):
        part = slice(h * size, (h + 1) * size)
        own_rate = rate[step * heads + h]
        decay = decay_matrix(own_rate)
        row = query_decay(own_rate, size)
        for b in range(blocks):
            span = slice(b * BLOCK, (b + 1) * BLOCK)
            q, k, v = query[span, part], keys[span, part], values[span, part]
            ab = backs[b][:, part]
            weights = (dot_nt(q, k) * decay).astype(BHALF)
            weights_back = (dot_nt(ab, v) * decay).astype(BHALF)
            value_part[span, part] = dot_tn(weights, ab)
            key_part[span, part] = dot_tn(weights_back, q)
            cot = dot_nn(weights_back, k) + row * dot_nt(ab, used[b][h])
            cot = unrotate(cot, cosine[span], sine[span])
            query_back[span, part] = (cot * swish_slope(pre_query[span, part])).astype(BHALF)


def query_side(rate, pre_query, query, keys, values, cosine, sine, backs, used, steps):
    tokens, width = query.shape
    heads = rate.shape[0]
    size = width // heads
    group = heads // steps
    cols = group * size
    blocks = len(backs)
    tile = pl.BlockSpec((tokens, cols), lambda i: (0, i))
    whole = lambda a: pl.BlockSpec(a.shape, lambda i: (0, 0))
    return call(
        functools.partial(query_body, group, blocks),
        (steps,),
        [SMEM_SPEC] + [tile] * 4 + [whole(cosine), whole(sine)]
        + [pl.BlockSpec((BLOCK, cols), lambda i: (0, i))] * blocks
        + [pl.BlockSpec((group, size, size), lambda i: (i, 0, 0))] * blocks,
        [tile] * 3,
        [shape_of(query.shape, d) for d in (BHALF, FLOAT, FLOAT)],
        12 * tokens * width * BLOCK,
        24 * tokens * width,
    )(rate, pre_query, query, keys, values, cosine, sine, *backs, *used)


def key_body(heads, blocks, rate, pre_key, keys, values, key_part, value_part, *refs):
    cosine, sine, state = refs[:3]
    direct = refs[3 : 3 + blocks]
    key_back, value_back = refs[3 + blocks :]
    step = pl.program_id(0)
    size = cosine.shape[1]
    for h in range(heads):
        part = slice(h * size, (h + 1) * size)
        own_rate = rate[step * heads + h]
        decay = key_decay(own_rate, size)
        here = state[h]
        for b in reversed(range(blocks)):
            span = slice(b * BLOCK, (b + 1) * BLOCK)
            used = here.astype(BHALF)
            cot = key_part[span, part] + decay * dot_nt(values[span, part], used)
            decayed = (keys[span, part].astype(FLOAT) * decay).astype(BHALF)
            vcot = value_part[span, part] + dot_nn(decayed, used)
            cot = unrotate(cot, cosine[span], sine[span])
            key_back[span, part] = (cot * swish_slope(pre_key[span, part])).astype(BHALF)
            value_back[span, part] = vcot.astype(BHALF)
            if b:
                here = scaled_by(-BLOCK * own_rate, here) + direct[b][h]


def key_side(rate, pre_key, keys, values, key_part, value_part, cosine, sine, state, direct, steps):
    tokens, width = keys.shape
    heads = rate.shape[0]
    size = width // heads
    group = heads // steps
    cols = group * size
    blocks = len(direct)
    tile = pl.BlockSpec((tokens, cols), lambda i: (0, i))
    whole = lambda a: pl.BlockSpec(a.shape, lambda i: (0, 0))
    cube = pl.BlockSpec((group, size, size), lambda i: (i, 0, 0))
    return call(
        functools.partial(key_body, group, blocks),
        (steps,),
        [SMEM_SPEC] + [tile] * 5 + [whole(cosine), whole(sine), cube] + [cube] * blocks,
        [tile] * 2,
        [shape_of(keys.shape, BHALF)] * 2,
        4 * tokens * width * size,
        20 * tokens * width,
    )(rate, pre_key, keys, values, key_part, value_part, cosine, sine, state, *direct)


def grads_body(lefts, pairs, core, *refs):
    left = refs[:lefts]
    right = refs[lefts:-2]
    keep, ship = refs[-2:]
    step = pl.program_id(0)
    for k, (l, rs) in enumerate(pairs):
        acc = None
        start = 0
        for piece in rs:
            r = right[piece]
            rows = r.shape[0]
            term = dot_tn(left[l][start : start + rows], r[...])
            start += rows
            acc = term if acc is None else acc + term

        @pl.when(step == 0)
        def _(acc=acc, k=k):
            keep[k] = acc.astype(BHALF)

        @pl.when(step == 1)
        def _(acc=acc, k=k):
            ship[k] = acc.astype(BHALF)


def grads(core, lefts, rights, pairs):
    tokens, width = lefts[0].shape
    cols = rights[0].shape[1]
    half = width // 2
    spec = pltpu.PrefetchScalarGridSpec(
        num_scalar_prefetch=1,
        grid=(2,),
        in_specs=[pl.BlockSpec((tokens, half), lambda i, c: (0, i ^ c[0]))] * len(lefts)
        + [pl.BlockSpec(r.shape, lambda i, c: (0, 0)) for r in rights],
        out_specs=[pl.BlockSpec((len(pairs), half, cols), lambda i, c: (0, 0, 0))] * 2,
    )
    n = len(pairs)
    body = functools.partial(grads_body, len(lefts), pairs)
    return pl.pallas_call(
        body,
        grid_spec=spec,
        out_shape=[shape_of((n, half, cols), BHALF)] * 2,
        cost_estimate=pl.CostEstimate(
            flops=2 * n * tokens * width * cols, bytes_accessed=4 * n * width * cols, transcendentals=0
        ),
        compiler_params=pltpu.CompilerParams(vmem_limit_bytes=VMEM_BYTES),
    )(core, *lefts, *rights)


def tokens_body(x, rc, qb, kb, vb, mb, wq, wk, wv, wm, out):
    grad = dot_nt(qb[...], wq[...]) + dot_nt(kb[...], wk[...])
    grad = grad + dot_nt(vb[...], wv[...]) + dot_nt(mb[...], wm[...])
    out[...] = rc[...] + srms_back(x[...].astype(FLOAT), grad)


def tokens_side(block, x, rc, qb, kb, vb, mb, weights):
    tokens, width = x.shape
    row = pl.BlockSpec((BLOCK, width), lambda i: (block, 0))
    own = pl.BlockSpec((BLOCK, width), lambda i: (0, 0))
    whole = pl.BlockSpec((width, width), lambda i: (0, 0))
    return call(
        tokens_body,
        (1,),
        [row, own, row, row, row, own] + [whole] * 4,
        own,
        shape_of((BLOCK, width), FLOAT),
        8 * BLOCK * width * width,
        8 * width * width + 20 * BLOCK * width,
    )(x, rc, qb, kb, vb, mb, *weights)


def angle_tables(position, halves):
    column = jnp.arange(halves, dtype=jnp.int32)
    factor = 1 + jnp.right_shift(jnp.full((halves,), 16384, jnp.int32), column // 4)
    phase = position[:, None] * factor[None, :] % 65536
    turned = phase.astype(FLOAT) * (2.0 * math.pi / 65536.0)
    cosine, sine = jnp.cos(turned), jnp.sin(turned)
    return jnp.concatenate([cosine, cosine], 1), jnp.concatenate([-sine, sine], 1)


def shards(
    tokens,
    query_weight,
    key_weight,
    value_weight,
    modulate_weight,
    output_weight,
    gate_weight,
    linear_weight,
    down_weight,
    cotangent,
    decay_exponent,
):
    count, width = tokens.shape
    heads = decay_exponent.shape[0]
    size = width // heads
    runs, members = lax.axis_size("seq"), lax.axis_size("tp")
    devices = runs * members
    length = min(SEQ_LEN, count * devices)
    span = length // count
    blocks = count // BLOCK
    seq_place = lax.axis_index("seq")
    place = seq_place * members + lax.axis_index("tp")
    core = bit_of(place, 1).astype(jnp.int32).reshape(1)
    position = (place * count + jnp.arange(count, dtype=jnp.int32)) % length
    rate = jnp.exp2(-decay_exponent.astype(FLOAT))
    cosine, sine = angle_tables(position, size // 2)
    ring = bits_of(members)
    far = ring[1:]

    normed, pre_key, keys, values, contrib, local = kv(
        rate, tokens, key_weight, value_weight, cosine, sine, 1
    )
    state, mark = decayed_scan(local, rate, float(count), span, place, False)
    pre_query, query, gate, intra = qu(
        rate, normed, query_weight, modulate_weight, cosine, sine, keys, values, 2
    )
    cots = gather_group(after(cotangent, mark), far + [1])
    joined = [
        join(b, rate, tokens, intra, query, gate, state, contrib, output_weight)
        for b in range(blocks)
    ]

    gate_t, linear_t = gate_weight.T, linear_weight.T
    gathered = [gather_group(joined[b][3], far + [1]) for b in range(blocks)]
    results = {}
    for r in range(0, members, 2):
        for b in range(blocks):
            results[r, b] = unit(
                b, gathered[b][r : r + 2], cots[r : r + 2], gate_t, linear_t, down_weight
            )
    groups = [
        tuple(gathered[b][r : r + 2]) + tuple(cots[r : r + 2]) + tuple(results[r, b][2:])
        for r in range(0, members, 2)
        for b in range(blocks)
    ]
    near = {}
    for key, value in results.items():
        near[key] = (value[0], swap(value[1], 1))
    arrived = {}
    for part in range(2):
        for b in range(blocks):
            rows = {
                r: near[r, b][0][part] + near[r, b][1][part].astype(FLOAT)
                for r in range(2, members, 2)
            }
            got = []
            for mask in reversed(far):
                for r in [r for r in rows if r & mask]:
                    value = swap(rows.pop(r).astype(BHALF), mask)
                    if r == mask:
                        got.append(value)
                    else:
                        rows[r ^ mask] = rows[r ^ mask] + value.astype(FLOAT)
            arrived[b, part] = got

    turned = [
        turn(
            b, rate, near[0, b][0], near[0, b][1], jnp.stack(arrived[b, 0]), joined[b][2],
            cotangent, joined[b][0], gate, query, output_weight,
        )
        for b in range(blocks)
    ]
    line = bits_of(runs)
    across = max(members // 2, 1)
    orders = (line, [m for m in line if m >= across] + [m for m in line if m < across])
    seq_scalar = seq_place.astype(jnp.int32).reshape(1)
    pair_part, down_part = unit_grads(seq_scalar, groups, orders, runs)

    decays = jnp.exp2(-BLOCK * rate)[:, None, None]
    inbound = turned[blocks - 1][4]
    for b in reversed(range(blocks - 1)):
        inbound = decays * inbound + turned[b][4]
    outer, _ = decayed_scan(inbound, rate, float(count), span, place, True)
    backs = [t[3] for t in turned]
    query_back, key_part, value_part = query_side(
        rate, pre_query, query, keys, values, cosine, sine, backs, [j[4] for j in joined], 2
    )
    rest = bits_of(devices)[1:]
    lines = [
        [m for m in rest if m < members],
        [m for m in rest if members <= m < members * across],
        [m for m in rest if m >= members * across],
    ]

    def order_of(k):
        return [m for i in range(3) for m in lines[(i + k) % 3]]

    def chip_sums(part):
        kept = (part[0].astype(FLOAT) + swap(part[1], 1).astype(FLOAT)).astype(BHALF)
        return [kept[k] for k in range(kept.shape[0])]

    def rest_of(piece, k, done):
        order = order_of(k)
        piece = double(halve(piece, order[done:], place), list(reversed(order)), place)
        return double(piece, [1], place).astype(FLOAT)

    gated = jnp.concatenate([j[1] for j in joined], axis=0)
    early = grads(
        core,
        [gated, normed],
        [t[1] for t in turned] + [t[2] for t in turned] + [query_back],
        [
            (0, list(range(blocks))),
            (1, list(range(blocks, 2 * blocks))),
            (1, [2 * blocks]),
        ],
    )
    moved = [halve(piece, order_of(k)[:1], place) for k, piece in enumerate(chip_sums(early))]
    key_back, value_back = key_side(
        rate, pre_key, keys, values, key_part, value_part, cosine, sine, outer,
        [t[4] for t in turned], 1,
    )
    late = grads(core, [normed], [key_back, value_back], [(0, [0]), (0, [1])])
    weights = (query_weight, key_weight, value_weight, modulate_weight)
    late_sums = chip_sums(late)
    late_moved = [halve(p, order_of(k)[:1], place) for k, p in enumerate(late_sums)]
    late_key = after(key_back, *late_sums)
    tokens_grad = jnp.concatenate(
        [
            tokens_side(
                b, tokens, turned[b][0], query_back, late_key, value_back, turned[b][2], weights
            )
            for b in range(blocks)
        ],
        axis=0,
    )

    mixed = jnp.concatenate(
        [
            (
                joined[b][2] + near[0, b][0][1] + near[0, b][1][1].astype(FLOAT)
                + sum(a.astype(FLOAT) for a in arrived[b, 1])
            ).astype(BHALF)
            for b in range(blocks)
        ],
        axis=0,
    )
    masks = [[members * m for m in order] for order in orders]
    pair_grad = fold(pair_part, masks[0]).astype(FLOAT)
    down_grad = fold(down_part, masks[1]).astype(FLOAT)
    gate_grad, linear_grad = pair_grad[0].T, pair_grad[1].T

    output_grad, modulate_grad, query_grad = [rest_of(p, k, 1) for k, p in enumerate(moved)]
    key_grad, value_grad = [rest_of(p, k, 1) for k, p in enumerate(late_moved)]
    return (
        mixed,
        tokens_grad,
        query_grad,
        key_grad,
        value_grad,
        modulate_grad,
        output_grad,
        gate_grad,
        linear_grad,
        down_grad,
    )


def solution(mesh):
    return jax.shard_map(
        shards,
        mesh=mesh,
        in_specs=(
            P(("seq", "tp"), None),
            P(),
            P(),
            P(),
            P(),
            P(),
            P(None, "tp"),
            P(None, "tp"),
            P("tp", None),
            P(("seq", "tp"), None),
            P(),
        ),
        out_specs=(
            P(("seq", "tp"), None),
            P(("seq", "tp"), None),
            P(),
            P(),
            P(),
            P(),
            P(),
            P("seq", "tp"),
            P("seq", "tp"),
            P("tp", "seq"),
        ),
        check_vma=False,
    )
```
